256 devices in a mesh: occi: 8 (over x_lo, y), occj: 32 (over z, x_hi, core).
Axes of the slice: x: 4 (x_hi: 2, x_lo: 2; x = x_hi * 2 + x_lo), y: 4, z: 8, core: 2. Of those that a mesh axis runs over, the one named last changes fastest.
Arguments:
- amplitudes: bfloat16 [64, 64, 256, 256], P('occi', 'occj'), may hold values from -6 to 6
- exchange: bfloat16 [64, 64, 256, 256], P('occi', 'occj'), may hold values from -6 to 6
- fock_virt: bfloat16 [256, 256], replicated, may hold values from -0.375 to 0.375
- intersection: bfloat16 [256, 256], replicated, may hold values from -0.1875 to 0.1875
- transform: bfloat16 [256, 256], replicated, may hold values from -0.375 to 0.375
- virt_energy: float32 [256], replicated, may hold values from 0.5 to 4
- occ_energy: float32 [64], replicated, may hold values from -1.5 to -0.3
- partners: int32 [64, 2], replicated, may hold values from 0 to 63, as said below
- coupling: float32 [64, 2], replicated, may hold values from -0.6 to 0.6
- domain: int32 [64, 8], replicated, may hold values 0 or 1
Outputs:
- residual: float32 [64, 64, 256, 256], P('occi', 'occj')
- new_amplitudes: bfloat16 [64, 64, 256, 256], P('occi', 'occj')
The draws below stay inside these ranges and needn't reach their ends.
Inputs may be any that keep to these rules, and one draw needn't show every extreme that they name: The 2 partners of orbital i are distinct, differ from i, and lie within 2 of i; the first lies exactly 2 away.
All inputs are finite; a program needn't handle non-finite values.
Results may differ from the reference program's by a relative error of at most 0.0085.
Values may be sent and summed in bfloat16 or wider, within the bound.
No kernel may reach another device: no remote copies, remote signals or barrier semaphores. Data moves between devices by JAX's collectives and lax.ppermute only.
A program may use at most 128 MiB of HBM per device.

```python
import math
import jax
import jax.numpy as jnp
from jax import lax

D = 256
NTILE = 8
REACH = 2
NP = 2
NO = 64


def draw_partners(key, part):
    key_sign = jax.random.fold_in(key, 11)
    key_pick = jax.random.fold_in(key, 23)
    rows = jnp.arange(NO, dtype=jnp.int32)
    sign = jax.random.randint(key_sign, (NO,), 0, 2).astype(jnp.int32) * 2 - 1
    sign = jnp.where(rows == REACH, -1, sign)
    sign = jnp.where(rows == NO - 1 - REACH, 1, sign)
    up_ok = rows + REACH < NO
    down_ok = rows - REACH >= 0
    sign = jnp.where(sign > 0, jnp.where(up_ok, 1, -1), jnp.where(down_ok, -1, 1)).astype(jnp.int32)
    first = rows + sign * REACH
    offsets = jnp.concatenate([jnp.arange(-REACH, 0), jnp.arange(1, REACH + 1)]).astype(jnp.int32)
    cands = offsets.shape[0]
    targets = rows[:, None] + offsets[None, :]
    valid = (targets >= 0) & (targets < NO) & (targets != first[:, None])
    noise = jax.random.randint(key_pick, (NO, cands), 0, 1 << 20).astype(jnp.int32)
    penalty = jnp.where(valid, 0, 1 << 26).astype(jnp.int32)
    scores = penalty + noise * cands + jnp.arange(cands, dtype=jnp.int32)[None, :]
    order = jnp.argsort(scores, axis=1)[:, :NP - 1]
    others = jnp.take_along_axis(targets, order, axis=1)
    return jnp.concatenate([first[:, None], others], axis=1).astype(jnp.int32)


def set_ends(array, key, least, high):
    extent = array.shape
    index_at = [jax.random.randint(jax.random.fold_in(key, axis), (), 0, extent[axis]) for axis in range(len(extent))]
    array = array.at[tuple(index_at)].set(least)
    longest = extent.index(max(extent))
    index_at[longest] = (index_at[longest] + 1) % extent[longest]
    return array.at[tuple(index_at)].set(high)


def steps_of(stream_key, extent, cuts, low, largest):
    gain, own = 1.0, jax.random.fold_in(stream_key, 6)
    for position, blocks in cuts:
        heights = jnp.exp(jax.random.uniform(jax.random.fold_in(own, position), (blocks,), jnp.float32, low / len(cuts), largest / len(cuts)))
        gain = gain * jnp.repeat(heights, extent[position] // blocks).reshape([-1 if axis == position else 1 for axis in range(len(extent))])
    return gain


def gaussian(stream_key, dims, spread, bound, pieces=(), kind=jnp.bfloat16):
    entries = jax.random.normal(stream_key, dims, jnp.float32) * spread
    if len(pieces) > 0:
        entries = steps_of(stream_key, dims, pieces, -0.22, 0.18) * entries
    return jnp.clip(entries, min=-bound, max=bound).astype(kind)


def setup_inputs(seed: int = 0) -> dict:
    splits = jax.random.split(jax.random.key(seed), 11)
    amplitudes = gaussian(splits[0], (NO, NO, D, D), 1.0, 6.0, ((0, 8), (1, 32)))
    exchange = gaussian(splits[1], (NO, NO, D, D), 1.0, 6.0, ((0, 8), (1, 32)))
    fock_virt = gaussian(splits[2], (D, D), D ** -0.5, 0.375)
    intersection = gaussian(splits[3], (D, D), (4 * D) ** -0.5, 0.1875)
    transform = gaussian(splits[4], (D, D), D ** -0.5, 0.375)
    virt_energy = jnp.clip(jnp.exp(jax.random.uniform(splits[5], (D,), jnp.float32, math.log(0.5), math.log(4.0))), 0.5, 4.0)
    occ_energy = jnp.clip(jax.random.uniform(splits[6], (NO,), jnp.float32, -1.5, -0.3), -1.5, -0.3)
    partners = draw_partners(jax.random.fold_in(splits[10], 71), 0)
    coupling = jnp.clip(jax.random.uniform(splits[8], (NO, NP), jnp.float32, -0.6, 0.6), -0.6, 0.6)
    domain = set_ends((jax.random.randint(splits[9], (NO, NTILE), 0, 3) < 2).astype(jnp.int32), jax.random.fold_in(splits[9], 1), 0, 1)
    return dict(amplitudes=amplitudes, exchange=exchange, fock_virt=fock_virt, intersection=intersection, transform=transform, virt_energy=virt_energy, occ_energy=occ_energy, partners=partners, coupling=coupling, domain=domain)


def rounded(value):
    return lax.optimization_barrier(value.astype(jnp.bfloat16)).astype(jnp.float32)


def reference(amplitudes, exchange, fock_virt, intersection, transform, virt_energy, occ_energy, partners, coupling, domain):
    count = amplitudes.shape[0]
    width = amplitudes.shape[2]
    tiles = domain.shape[1]
    numbers = jnp.arange(count, dtype=jnp.int32)
    intersection_full = (jnp.eye(width, dtype=jnp.float32) + intersection.astype(jnp.float32)).astype(jnp.bfloat16)
    over32 = intersection_full.astype(jnp.float32)
    fock32 = fock_virt.astype(jnp.float32)
    trans32 = transform.astype(jnp.float32)

    def sym_row(index):
        own = lax.dynamic_index_in_dim(amplitudes, index, 0, keepdims=False).astype(jnp.float32)
        other = lax.dynamic_index_in_dim(amplitudes, index, 1, keepdims=False)
        return (0.5 * (own + jnp.transpose(other, (0, 2, 1)).astype(jnp.float32))).astype(jnp.bfloat16)

    sym = lax.map(sym_row, numbers)

    def coupled_row(index):
        total = jnp.zeros((count, width, width), jnp.float32)
        for slot in range(partners.shape[1]):
            other = partners[index, slot].astype(jnp.int32)
            total = total + coupling[index, slot] * lax.dynamic_index_in_dim(sym, other, 0, keepdims=False).astype(jnp.float32)
        return total.astype(jnp.bfloat16)

    c_row = lax.map(coupled_row, numbers)
    masks = jnp.repeat(domain.astype(jnp.float32), width // tiles, axis=1)

    def row_step(index):
        amps = lax.dynamic_index_in_dim(amplitudes, index, 0, keepdims=False).astype(jnp.float32)
        exch = lax.dynamic_index_in_dim(exchange, index, 0, keepdims=False).astype(jnp.float32)
        own_row = lax.dynamic_index_in_dim(c_row, index, 0, keepdims=False).astype(jnp.float32)
        own_col = lax.dynamic_index_in_dim(c_row, index, 1, keepdims=False)
        coup = own_row + jnp.transpose(own_col, (0, 2, 1)).astype(jnp.float32)
        mask_i = lax.dynamic_index_in_dim(masks, index, 0, keepdims=False)
        mpair = jnp.maximum(mask_i[None, :], masks)
        two = mpair[:, :, None] * mpair[:, None, :]
        cmask = rounded(coup * two)
        a1 = rounded(jnp.einsum('ab,jbc->jac', fock32, amps))
        first = jnp.einsum('jab,bc->jac', a1, over32)
        a2 = rounded(jnp.einsum('ab,jbc->jac', over32, amps))
        second = jnp.einsum('jab,bc->jac', a2, fock32)
        b1 = rounded(jnp.einsum('ab,jbc->jac', over32, cmask))
        third = jnp.einsum('jab,bc->jac', b1, over32)
        resid = two * (exch + first + second - third)
        resid_b = rounded(resid)
        q1 = rounded(jnp.einsum('ba,jbc->jac', trans32, resid_b))
        q2 = jnp.einsum('jab,bc->jac', q1, trans32)
        occ_i = lax.dynamic_index_in_dim(occ_energy, index, 0, keepdims=False)
        denom = virt_energy[None, :, None] + virt_energy[None, None, :] - occ_i - occ_energy[:, None, None]
        zeta = rounded(q2 / denom)
        u1 = rounded(jnp.einsum('ab,jbc->jac', trans32, zeta))
        u2 = jnp.einsum('jab,cb->jac', u1, trans32)
        fresh = (amps - u2).astype(jnp.bfloat16)
        return resid, fresh

    resid_all, fresh_all = lax.map(row_step, numbers)
    return resid_all, fresh_all
```

```python
import functools

import jax
import jax.numpy as jnp
from jax import lax
from jax.experimental import pallas as pl
from jax.experimental.pallas import tpu as pltpu
from jax.sharding import Mesh
from jax.sharding import PartitionSpec as P

REACH = 2
SR = 16
SL = 128


def _cut(block):
    w = block.shape[0]
    parts = [
        block[SR * u : SR * u + SR, SL * v : SL * v + SL][None]
        for u in range(w // SR)
        for v in range(w // SL)
    ]
    return jnp.concatenate(parts, axis=0)


def _glue(slabs, w):
    halves = w // SL
    cols = [
        jnp.concatenate([slabs[u * halves + v] for u in range(w // SR)], axis=0)
        for v in range(halves)
    ]
    return jnp.concatenate(cols, axis=1)


def pack_kernel(x_ref, o_ref, *, flip):
    for r in range(x_ref.shape[0]):
        for s in range(x_ref.shape[1]):
            block = x_ref[r, s]
            if flip:
                block = block.astype(jnp.float32).T.astype(jnp.bfloat16)
            w = block.shape[0]
            for u in range(w // SR):
                for v in range(w // SL):
                    o_ref[u * (w // SL) + v, r, s] = block[
                        SR * u : SR * u + SR, SL * v : SL * v + SL
                    ]


def pack(x, flip):
    rows, cols, w, _ = x.shape
    n = (w // SR) * (w // SL)
    step = 2
    return pl.pallas_call(
        functools.partial(pack_kernel, flip=flip),
        grid=(rows // step,),
        in_specs=[pl.BlockSpec((step, cols, w, w), lambda k: (k, 0, 0, 0))],
        out_specs=pl.BlockSpec((n, step, cols, SR, SL), lambda k: (0, k, 0, 0, 0)),
        out_shape=jax.ShapeDtypeStruct((n, rows, cols, SR, SL), jnp.bfloat16),
        name="pack_flip" if flip else "pack",
    )(x)


def sym_kernel(a_ref, b_ref, o_ref, lo_ref, hi_ref):
    _, g_n, r_n, s_n, _, _ = a_ref.shape
    j_n = g_n * s_n
    for g in range(g_n):
        for s in range(s_n):
            j = g * s_n + s
            for i in range(r_n):
                own = a_ref[0, g, i, s].astype(jnp.float32)
                mir = b_ref[0, i // s_n, j, i % s_n].astype(jnp.float32)
                val = (0.5 * (own + mir)).astype(jnp.bfloat16)
                o_ref[j, i] = val
                if j < REACH:
                    lo_ref[j, i] = val
                if j >= j_n - REACH:
                    hi_ref[j - j_n + REACH, i] = val


def symmetrize(a, b):
    t_n, g_n, r_n, s_n, _, _ = a.shape
    j_n = g_n * s_n
    spec = pl.BlockSpec((1, g_n, r_n, s_n, SR, SL), lambda t: (t, 0, 0, 0, 0, 0))
    out = lambda n: pl.BlockSpec((n, r_n, SR, SL), lambda t: (0, t, 0, 0))
    shape = lambda n: jax.ShapeDtypeStruct((n, t_n * r_n, SR, SL), jnp.bfloat16)
    return pl.pallas_call(
        sym_kernel,
        grid=(t_n,),
        in_specs=[spec, spec],
        out_specs=[out(j_n), out(REACH), out(REACH)],
        out_shape=[shape(j_n), shape(REACH), shape(REACH)],
        name="sym",
    )(a, b)


def coup_kernel(
    lists_ref, weights_ref, start_ref, sym_ref, left_ref, right_ref, o_ref, ext_ref, sems
):
    t = pl.program_id(0)
    j_n = sym_ref.shape[0]
    copies = [
        pltpu.make_async_copy(left_ref, ext_ref.at[pl.ds(0, REACH)], sems.at[0]),
        pltpu.make_async_copy(sym_ref, ext_ref.at[pl.ds(REACH, j_n)], sems.at[1]),
        pltpu.make_async_copy(right_ref, ext_ref.at[pl.ds(REACH + j_n, REACH)], sems.at[2]),
    ]

    @pl.when(t == 0)
    def _():
        for c in copies:
            c.start()
        for c in copies:
            c.wait()

    _, g_n, r_n, s_n, _, _ = o_ref.shape
    start = start_ref[0]
    for j in range(j_n):
        gj = start + j
        p0 = lists_ref[gj, 0] - start + REACH
        p1 = lists_ref[gj, 1] - start + REACH
        w0 = weights_ref[gj, 0]
        w1 = weights_ref[gj, 1]
        for r in range(r_n):
            i = t * r_n + r
            row = weights_ref[i, 0] * ext_ref[j + REACH, lists_ref[i, 0]].astype(jnp.float32)
            row = row + weights_ref[i, 1] * ext_ref[j + REACH, lists_ref[i, 1]].astype(jnp.float32)
            col = w0 * ext_ref[p0, i].astype(jnp.float32)
            col = col + w1 * ext_ref[p1, i].astype(jnp.float32)
            total = row.astype(jnp.bfloat16).astype(jnp.float32) + col.astype(jnp.bfloat16).astype(
                jnp.float32
            )
            o_ref[0, j // s_n, r, j % s_n] = total.astype(jnp.bfloat16)


def couple(lists, weights, start, sym, left, right, r_n, s_n):
    j_n, i_n = sym.shape[:2]
    g_n = j_n // s_n
    t_n = i_n // r_n
    hbm = pl.BlockSpec(memory_space=pl.ANY)
    return pl.pallas_call(
        coup_kernel,
        grid_spec=pltpu.PrefetchScalarGridSpec(
            num_scalar_prefetch=3,
            grid=(t_n,),
            in_specs=[hbm, hbm, hbm],
            out_specs=pl.BlockSpec((1, g_n, r_n, s_n, SR, SL), lambda t, *_: (t, 0, 0, 0, 0, 0)),
            scratch_shapes=[
                pltpu.VMEM((j_n + 2 * REACH, i_n, SR, SL), jnp.bfloat16),
                pltpu.SemaphoreType.DMA((3,)),
            ],
        ),
        out_shape=jax.ShapeDtypeStruct((t_n, g_n, r_n, s_n, SR, SL), jnp.bfloat16),
        name="couple",
    )(lists, weights, start, sym, left, right)


def _dot(x, y):
    return jnp.dot(x, y, preferred_element_type=jnp.float32)


def pre_kernel(amp_ref, exch_ref, fock_ref, over_ref, o_ref):
    fock = fock_ref[...]
    over = over_ref[...]
    for s in range(amp_ref.shape[1]):
        amp = amp_ref[0, s]
        first = _dot(_dot(fock, amp).astype(jnp.bfloat16), over)
        second = _dot(_dot(over, amp).astype(jnp.bfloat16), fock)
        o_ref[0, s] = exch_ref[0, s].astype(jnp.float32) + first + second


def precompute(amp, exch, fock, over):
    rows, cols, w, _ = amp.shape
    big = pl.BlockSpec((1, cols, w, w), lambda k: (k, 0, 0, 0))
    mat = pl.BlockSpec((w, w), lambda k: (0, 0))
    return pl.pallas_call(
        pre_kernel,
        grid=(rows,),
        in_specs=[big, big, mat, mat],
        out_specs=big,
        out_shape=jax.ShapeDtypeStruct(amp.shape, jnp.float32),
        name="precompute",
    )(amp, exch, fock, over)


def post_kernel(
    occ_ref,
    base_ref,
    amp_ref,
    coup_ref,
    mrow_i_ref,
    mrow_j_ref,
    mcol_i_ref,
    mcol_j_ref,
    over_ref,
    trans_ref,
    tt_ref,
    erow_ref,
    ecol_ref,
    res_ref,
    new_ref,
):
    k = pl.program_id(0)
    w = amp_ref.shape[2]
    rows = pl.num_programs(0)
    over = over_ref[...]
    trans = trans_ref[...]
    tt = tt_ref[...]
    for s in range(amp_ref.shape[1]):
        row = jnp.maximum(mrow_i_ref[0], mrow_j_ref[s])
        col = jnp.maximum(mcol_i_ref[0], mcol_j_ref[s])
        two = col * row
        cm = (_glue([coup_ref[n, 0, s] for n in range(coup_ref.shape[0])], w).astype(jnp.float32) * two).astype(
            jnp.bfloat16
        )
        third = _dot(_dot(over, cm).astype(jnp.bfloat16), over)
        res = two * (base_ref[0, s] - third)
        res_ref[0, s] = res
        q = _dot(_dot(tt, res.astype(jnp.bfloat16)).astype(jnp.bfloat16), trans)
        denom = ecol_ref[...] + erow_ref[...] - (occ_ref[k] + occ_ref[rows + s])
        z = (q / denom).astype(jnp.bfloat16)
        u = _dot(_dot(trans, z).astype(jnp.bfloat16), tt)
        new_ref[0, s] = (amp_ref[0, s].astype(jnp.float32) - u).astype(jnp.bfloat16)


def finish(occ, base, amp, coup, mask_i, mask_j, over, trans, energy):
    rows, cols, w, _ = amp.shape
    n = coup.shape[0]
    big = pl.BlockSpec((1, cols, w, w), lambda k, *_: (k, 0, 0, 0))
    mat = pl.BlockSpec((w, w), lambda k, *_: (0, 0))
    return pl.pallas_call(
        post_kernel,
        grid_spec=pltpu.PrefetchScalarGridSpec(
            num_scalar_prefetch=1,
            grid=(rows,),
            in_specs=[
                big,
                big,
                pl.BlockSpec((n, 1, cols, SR, SL), lambda k, *_: (0, k, 0, 0, 0)),
                pl.BlockSpec((1, 1, w), lambda k, *_: (k, 0, 0)),
                pl.BlockSpec((cols, 1, w), lambda k, *_: (0, 0, 0)),
                pl.BlockSpec((1, w, 1), lambda k, *_: (k, 0, 0)),
                pl.BlockSpec((cols, w, 1), lambda k, *_: (0, 0, 0)),
                mat,
                mat,
                mat,
                pl.BlockSpec((1, w), lambda k, *_: (0, 0)),
                pl.BlockSpec((w, 1), lambda k, *_: (0, 0)),
            ],
            out_specs=[big, big],
        ),
        out_shape=[
            jax.ShapeDtypeStruct(amp.shape, jnp.float32),
            jax.ShapeDtypeStruct(amp.shape, jnp.bfloat16),
        ],
        name="finish",
    )(
        occ,
        base,
        amp,
        coup,
        mask_i[:, None, :],
        mask_j[:, None, :],
        mask_i[:, :, None],
        mask_j[:, :, None],
        over,
        trans,
        trans.T,
        energy[None, :],
        energy[:, None],
    )


def per_device(
    amplitudes,
    exchange,
    fock_virt,
    intersection,
    transform,
    virt_energy,
    occ_energy,
    partners,
    coupling,
    domain,
):
    rows, cols, width, _ = amplitudes.shape
    tiles = domain.shape[1]
    a_n = lax.axis_size("a")
    z_n = lax.axis_size("z")
    g_n = lax.axis_size("g")
    start_i = lax.axis_index("a") * rows
    start_z = lax.axis_index("z") * (g_n * cols)
    start_j = start_z + lax.axis_index("g") * cols
    plane = ("a", "g")
    n = a_n * g_n

    over = (jnp.eye(width, dtype=jnp.float32) + intersection.astype(jnp.float32)).astype(
        jnp.bfloat16
    )
    flipped = pack(amplitudes, True)
    flipped = lax.all_to_all(flipped, plane, 0, 0, tiled=True)
    flipped = lax.all_to_all(flipped, "z", 0, 0, tiled=True)
    own = lax.all_to_all(pack(amplitudes, False), plane, 0, 0, tiled=True)
    shape = (a_n, g_n, rows, cols, SR, SL)
    sym, low, high = symmetrize(own.reshape(shape), flipped.reshape(shape))
    up = [(k, k + 1) for k in range(z_n - 1)]
    down = [(k + 1, k) for k in range(z_n - 1)]
    left = lax.ppermute(high, "z", up)
    right = lax.ppermute(low, "z", down)
    base = precompute(amplitudes, exchange, fock_virt, over)
    coup = couple(partners, coupling, start_z[None], sym, left, right, rows, cols)
    coup = lax.all_to_all(coup.reshape(n, rows, cols, SR, SL), plane, 0, 0, tiled=True)

    masks = jnp.repeat(domain.astype(jnp.float32), width // tiles, axis=1)
    mask_i = lax.dynamic_slice_in_dim(masks, start_i, rows, 0)
    mask_j = lax.dynamic_slice_in_dim(masks, start_j, cols, 0)
    occ = jnp.concatenate(
        [
            lax.dynamic_slice_in_dim(occ_energy, start_i, rows, 0),
            lax.dynamic_slice_in_dim(occ_energy, start_j, cols, 0),
        ]
    )
    return tuple(
        finish(occ, base, amplitudes, coup, mask_i, mask_j, over, transform, virt_energy)
    )


def solution(mesh):
    i_n, j_n = mesh.shape["occi"], mesh.shape["occj"]
    group = j_n // i_n
    inner = Mesh(mesh.devices.reshape(i_n, j_n // group, group), ("a", "z", "g"))
    pairs = P("a", ("z", "g"), None, None)
    return jax.shard_map(
        per_device,
        mesh=inner,
        in_specs=(pairs, pairs, P(), P(), P(), P(), P(), P(), P(), P()),
        out_specs=(pairs, pairs),
        check_vma=False,
    )
```

```python
import functools

import jax
import jax.numpy as jnp
from jax import lax
from jax.experimental import pallas as pl
from jax.experimental.pallas import tpu as pltpu
from jax.sharding import Mesh
from jax.sharding import PartitionSpec as P

REACH = 2
SR = 16
SL = 128


def _cut(block):
    w = block.shape[0]
    parts = [
        block[SR * u : SR * u + SR, SL * v : SL * v + SL][None]
        for u in range(w // SR)
        for v in range(w // SL)
    ]
    return jnp.concatenate(parts, axis=0)


def _glue(slabs, w):
    halves = w // SL
    cols = [
        jnp.concatenate([slabs[u * halves + v] for u in range(w // SR)], axis=0)
        for v in range(halves)
    ]
    return jnp.concatenate(cols, axis=1)


def pack_kernel(x_ref, o_ref, *, flip):
    for r in range(x_ref.shape[0]):
        for s in range(x_ref.shape[1]):
            block = x_ref[r, s]
            if flip:
                block = block.astype(jnp.float32).T.astype(jnp.bfloat16)
            w = block.shape[0]
            for u in range(w // SR):
                for v in range(w // SL):
                    o_ref[u * (w // SL) + v, r, s] = block[
                        SR * u : SR * u + SR, SL * v : SL * v + SL
                    ]


def pack(x, flip):
    rows, cols, w, _ = x.shape
    n = (w // SR) * (w // SL)
    step = 2
    return pl.pallas_call(
        functools.partial(pack_kernel, flip=flip),
        grid=(rows // step,),
        in_specs=[pl.BlockSpec((step, cols, w, w), lambda k: (k, 0, 0, 0))],
        out_specs=pl.BlockSpec((n, step, cols, SR, SL), lambda k: (0, k, 0, 0, 0)),
        out_shape=jax.ShapeDtypeStruct((n, rows, cols, SR, SL), jnp.bfloat16),
        name="pack_flip" if flip else "pack",
    )(x)


def sym_kernel(z_ref, a_ref, *refs):
    t_n = pl.num_programs(0)
    k = pl.program_id(0)
    got, (o_ref, lo_ref, hi_ref, b_ref, sems) = refs[:-5], refs[-5:]
    copies = [pltpu.make_async_copy(x, b_ref.at[q], sems.at[q]) for q, x in enumerate(got)]

    @pl.when(k == 0)
    def _():
        for c in copies:
            c.start()

    for q, c in enumerate(copies):

        @pl.when(k == q)
        def _(c=c):
            c.wait()

    _, g_n, r_n, s_n, _, _ = a_ref.shape
    j_n = g_n * s_n
    for g in range(g_n):
        for s in range(s_n):
            j = g * s_n + s
            for i in range(r_n):
                own = a_ref[0, g, i, s].astype(jnp.float32)
                mir = b_ref[k, i // s_n, j, i % s_n].astype(jnp.float32)
                val = (0.5 * (own + mir)).astype(jnp.bfloat16)
                o_ref[j, i] = val
                if j < REACH:
                    lo_ref[j, i] = val
                if j >= j_n - REACH:
                    hi_ref[j - j_n + REACH, i] = val


def symmetrize(z, own, got):
    t_n, g_n, r_n, s_n, _, _ = own.shape
    j_n = g_n * s_n
    tile = lambda k, z_ref: lax.rem(z_ref[0] - k + t_n, t_n)
    spec = pl.BlockSpec((1, g_n, r_n, s_n, SR, SL), lambda k, z: (tile(k, z), 0, 0, 0, 0, 0))
    out = lambda n: pl.BlockSpec((n, r_n, SR, SL), lambda k, z: (0, tile(k, z), 0, 0))
    shape = lambda n: jax.ShapeDtypeStruct((n, t_n * r_n, SR, SL), jnp.bfloat16)
    hbm = pl.BlockSpec(memory_space=pl.ANY)
    return pl.pallas_call(
        sym_kernel,
        grid_spec=pltpu.PrefetchScalarGridSpec(
            num_scalar_prefetch=1,
            grid=(t_n,),
            in_specs=[spec] + [hbm] * t_n,
            out_specs=[out(j_n), out(REACH), out(REACH)],
            scratch_shapes=[
                pltpu.VMEM(own.shape, jnp.bfloat16),
                pltpu.SemaphoreType.DMA((t_n,)),
            ],
        ),
        out_shape=[shape(j_n), shape(REACH), shape(REACH)],
        name="sym",
    )(z[None], own, *got)


def coup_kernel(
    lists_ref, weights_ref, start_ref, sym_ref, left_ref, right_ref, o_ref, ext_ref, sems
):
    t = pl.program_id(0)
    j_n = sym_ref.shape[0]
    copies = [
        pltpu.make_async_copy(left_ref, ext_ref.at[pl.ds(0, REACH)], sems.at[0]),
        pltpu.make_async_copy(sym_ref, ext_ref.at[pl.ds(REACH, j_n)], sems.at[1]),
        pltpu.make_async_copy(right_ref, ext_ref.at[pl.ds(REACH + j_n, REACH)], sems.at[2]),
    ]

    @pl.when(t == 0)
    def _():
        for c in copies:
            c.start()
        for c in copies:
            c.wait()

    _, g_n, r_n, s_n, _, _ = o_ref.shape
    start = start_ref[0]
    for j in range(j_n):
        gj = start + j
        p0 = lists_ref[gj, 0] - start + REACH
        p1 = lists_ref[gj, 1] - start + REACH
        w0 = weights_ref[gj, 0]
        w1 = weights_ref[gj, 1]
        for r in range(r_n):
            i = t * r_n + r
            row = weights_ref[i, 0] * ext_ref[j + REACH, lists_ref[i, 0]].astype(jnp.float32)
            row = row + weights_ref[i, 1] * ext_ref[j + REACH, lists_ref[i, 1]].astype(jnp.float32)
            col = w0 * ext_ref[p0, i].astype(jnp.float32)
            col = col + w1 * ext_ref[p1, i].astype(jnp.float32)
            total = row.astype(jnp.bfloat16).astype(jnp.float32) + col.astype(jnp.bfloat16).astype(
                jnp.float32
            )
            o_ref[0, j // s_n, r, j % s_n] = total.astype(jnp.bfloat16)


def couple(lists, weights, start, sym, left, right, r_n, s_n):
    j_n, i_n = sym.shape[:2]
    g_n = j_n // s_n
    t_n = i_n // r_n
    hbm = pl.BlockSpec(memory_space=pl.ANY)
    return pl.pallas_call(
        coup_kernel,
        grid_spec=pltpu.PrefetchScalarGridSpec(
            num_scalar_prefetch=3,
            grid=(t_n,),
            in_specs=[hbm, hbm, hbm],
            out_specs=pl.BlockSpec((1, g_n, r_n, s_n, SR, SL), lambda t, *_: (t, 0, 0, 0, 0, 0)),
            scratch_shapes=[
                pltpu.VMEM((j_n + 2 * REACH, i_n, SR, SL), jnp.bfloat16),
                pltpu.SemaphoreType.DMA((3,)),
            ],
        ),
        out_shape=jax.ShapeDtypeStruct((t_n, g_n, r_n, s_n, SR, SL), jnp.bfloat16),
        name="couple",
    )(lists, weights, start, sym, left, right)


def _dot(x, y):
    return jnp.dot(x, y, preferred_element_type=jnp.float32)


def pre_kernel(amp_ref, exch_ref, fock_ref, over_ref, o_ref):
    fock = fock_ref[...]
    over = over_ref[...]
    for s in range(amp_ref.shape[1]):
        amp = amp_ref[0, s]
        first = _dot(_dot(fock, amp).astype(jnp.bfloat16), over)
        second = _dot(_dot(over, amp).astype(jnp.bfloat16), fock)
        o_ref[0, s] = exch_ref[0, s].astype(jnp.float32) + first + second


def precompute(amp, exch, fock, over):
    rows, cols, w, _ = amp.shape
    big = pl.BlockSpec((1, cols, w, w), lambda k: (k, 0, 0, 0))
    mat = pl.BlockSpec((w, w), lambda k: (0, 0))
    return pl.pallas_call(
        pre_kernel,
        grid=(rows,),
        in_specs=[big, big, mat, mat],
        out_specs=big,
        out_shape=jax.ShapeDtypeStruct(amp.shape, jnp.float32),
        name="precompute",
    )(amp, exch, fock, over)


def post_kernel(
    occ_ref,
    base_ref,
    amp_ref,
    coup_ref,
    mrow_i_ref,
    mrow_j_ref,
    mcol_i_ref,
    mcol_j_ref,
    over_ref,
    trans_ref,
    tt_ref,
    erow_ref,
    ecol_ref,
    res_ref,
    new_ref,
):
    k = pl.program_id(0)
    w = amp_ref.shape[2]
    rows = pl.num_programs(0)
    over = over_ref[...]
    trans = trans_ref[...]
    tt = tt_ref[...]
    for s in range(amp_ref.shape[1]):
        row = jnp.maximum(mrow_i_ref[0], mrow_j_ref[s])
        col = jnp.maximum(mcol_i_ref[0], mcol_j_ref[s])
        two = col * row
        cm = (_glue([coup_ref[n, 0, s] for n in range(coup_ref.shape[0])], w).astype(jnp.float32) * two).astype(
            jnp.bfloat16
        )
        third = _dot(_dot(over, cm).astype(jnp.bfloat16), over)
        res = two * (base_ref[0, s] - third)
        res_ref[0, s] = res
        q = _dot(_dot(tt, res.astype(jnp.bfloat16)).astype(jnp.bfloat16), trans)
        denom = ecol_ref[...] + erow_ref[...] - (occ_ref[k] + occ_ref[rows + s])
        z = (q / denom).astype(jnp.bfloat16)
        u = _dot(_dot(trans, z).astype(jnp.bfloat16), tt)
        new_ref[0, s] = (amp_ref[0, s].astype(jnp.float32) - u).astype(jnp.bfloat16)


def finish(occ, base, amp, coup, mask_i, mask_j, over, trans, energy):
    rows, cols, w, _ = amp.shape
    n = coup.shape[0]
    big = pl.BlockSpec((1, cols, w, w), lambda k, *_: (k, 0, 0, 0))
    mat = pl.BlockSpec((w, w), lambda k, *_: (0, 0))
    return pl.pallas_call(
        post_kernel,
        grid_spec=pltpu.PrefetchScalarGridSpec(
            num_scalar_prefetch=1,
            grid=(rows,),
            in_specs=[
                big,
                big,
                pl.BlockSpec((n, 1, cols, SR, SL), lambda k, *_: (0, k, 0, 0, 0)),
                pl.BlockSpec((1, 1, w), lambda k, *_: (k, 0, 0)),
                pl.BlockSpec((cols, 1, w), lambda k, *_: (0, 0, 0)),
                pl.BlockSpec((1, w, 1), lambda k, *_: (k, 0, 0)),
                pl.BlockSpec((cols, w, 1), lambda k, *_: (0, 0, 0)),
                mat,
                mat,
                mat,
                pl.BlockSpec((1, w), lambda k, *_: (0, 0)),
                pl.BlockSpec((w, 1), lambda k, *_: (0, 0)),
            ],
            out_specs=[big, big],
        ),
        out_shape=[
            jax.ShapeDtypeStruct(amp.shape, jnp.float32),
            jax.ShapeDtypeStruct(amp.shape, jnp.bfloat16),
        ],
        name="finish",
    )(
        occ,
        base,
        amp,
        coup,
        mask_i[:, None, :],
        mask_j[:, None, :],
        mask_i[:, :, None],
        mask_j[:, :, None],
        over,
        trans,
        trans.T,
        energy[None, :],
        energy[:, None],
    )


def per_device(
    amplitudes,
    exchange,
    fock_virt,
    intersection,
    transform,
    virt_energy,
    occ_energy,
    partners,
    coupling,
    domain,
):
    rows, cols, width, _ = amplitudes.shape
    tiles = domain.shape[1]
    a_n = lax.axis_size("a")
    z_n = lax.axis_size("z")
    g_n = lax.axis_size("g")
    start_i = lax.axis_index("a") * rows
    start_z = lax.axis_index("z") * (g_n * cols)
    start_j = start_z + lax.axis_index("g") * cols
    plane = ("a", "g")
    n = a_n * g_n

    over = (jnp.eye(width, dtype=jnp.float32) + intersection.astype(jnp.float32)).astype(
        jnp.bfloat16
    )
    flipped = pack(amplitudes, True)
    flipped = lax.all_to_all(flipped, plane, 0, 0, tiled=True)
    flipped, own = lax.optimization_barrier((flipped, pack(amplitudes, False)))
    shape = (a_n, g_n, rows, cols, SR, SL)
    flipped = flipped.reshape(shape)
    z = lax.axis_index("z")
    got = []
    for k in range(z_n):
        part = lax.dynamic_index_in_dim(flipped, lax.rem(z + k, z_n), 0, keepdims=False)
        if k:
            part = lax.ppermute(part, "z", [(q, (q + k) % z_n) for q in range(z_n)])
        got.append(part)
    own = lax.all_to_all(own, plane, 0, 0, tiled=True)
    sym, low, high = symmetrize(z, own.reshape(shape), got)
    up = [(k, k + 1) for k in range(z_n - 1)]
    down = [(k + 1, k) for k in range(z_n - 1)]
    left = lax.ppermute(high, "z", up)
    right = lax.ppermute(low, "z", down)
    base = precompute(amplitudes, exchange, fock_virt, over)
    coup = couple(partners, coupling, start_z[None], sym, left, right, rows, cols)
    coup = lax.all_to_all(coup.reshape(n, rows, cols, SR, SL), plane, 0, 0, tiled=True)

    masks = jnp.repeat(domain.astype(jnp.float32), width // tiles, axis=1)
    mask_i = lax.dynamic_slice_in_dim(masks, start_i, rows, 0)
    mask_j = lax.dynamic_slice_in_dim(masks, start_j, cols, 0)
    occ = jnp.concatenate(
        [
            lax.dynamic_slice_in_dim(occ_energy, start_i, rows, 0),
            lax.dynamic_slice_in_dim(occ_energy, start_j, cols, 0),
        ]
    )
    return tuple(
        finish(occ, base, amplitudes, coup, mask_i, mask_j, over, transform, virt_energy)
    )


def solution(mesh):
    i_n, j_n = mesh.shape["occi"], mesh.shape["occj"]
    group = j_n // i_n
    inner = Mesh(mesh.devices.reshape(i_n, j_n // group, group), ("a", "z", "g"))
    pairs = P("a", ("z", "g"), None, None)
    return jax.shard_map(
        per_device,
        mesh=inner,
        in_specs=(pairs, pairs, P(), P(), P(), P(), P(), P(), P(), P()),
        out_specs=(pairs, pairs),
        check_vma=False,
    )
```

```python
import functools

import jax
import jax.numpy as jnp
from jax import lax
from jax.experimental import pallas as pl
from jax.experimental.pallas import tpu as pltpu
from jax.sharding import Mesh
from jax.sharding import PartitionSpec as P

REACH = 2
CHUNKS = 2
VMEM = pl.BlockSpec(memory_space=pltpu.VMEM)
SMEM = pl.BlockSpec(memory_space=pltpu.SMEM)


def pack_kernel(x_ref, *o_refs, flip):
    n, _, _, sr, sl = o_refs[0].shape
    for r in range(x_ref.shape[0]):
        for s in range(x_ref.shape[1]):
            block = x_ref[r, s].astype(jnp.float32)
            if flip:
                block = block.T
            for h, o_ref in enumerate(o_refs):
                for u in range(n):
                    o_ref[u, r, s] = block[sr * u : sr * u + sr, sl * h : sl * h + sl].astype(
                        jnp.bfloat16
                    )


def pack(x, n, flip):
    rows, cols, w, _ = x.shape
    sr, sl = w // n, w // CHUNKS
    step = 2
    return pl.pallas_call(
        functools.partial(pack_kernel, flip=flip),
        grid=(rows // step,),
        in_specs=[pl.BlockSpec((step, cols, w, w), lambda k: (k, 0, 0, 0))],
        out_specs=[pl.BlockSpec((n, step, cols, sr, sl), lambda k: (0, k, 0, 0, 0))] * CHUNKS,
        out_shape=[jax.ShapeDtypeStruct((n, rows, cols, sr, sl), jnp.bfloat16)] * CHUNKS,
        name="pack_flip" if flip else "pack",
    )(x)


def sym_kernel(z_ref, a_ref, *refs):
    got, (o_ref, lo_ref, hi_ref) = refs[:-3], refs[-3:]
    t_n, g_n, r_n, s_n, _, _ = a_ref.shape
    j_n = g_n * s_n
    for k, b_ref in enumerate(got):
        t = lax.rem(z_ref[0] + (t_n - k), t_n)
        for j in range(j_n):
            for i in range(r_n):
                own = a_ref[t, j // s_n, i, j % s_n].astype(jnp.float32)
                mir = b_ref[i // s_n, j, i % s_n].astype(jnp.float32)
                val = (0.5 * (own + mir)).astype(jnp.bfloat16)
                o_ref[j, t * r_n + i] = val
                if j < REACH:
                    lo_ref[j, t * r_n + i] = val
                if j >= j_n - REACH:
                    hi_ref[j - j_n + REACH, t * r_n + i] = val


def symmetrize(z, own, got):
    t_n, g_n, r_n, s_n, sr, sl = own.shape
    shape = lambda n: jax.ShapeDtypeStruct((n, t_n * r_n, sr, sl), jnp.bfloat16)
    return pl.pallas_call(
        sym_kernel,
        in_specs=[SMEM, VMEM] + [VMEM] * len(got),
        out_specs=[VMEM] * 3,
        out_shape=[shape(g_n * s_n), shape(REACH), shape(REACH)],
        name="sym",
    )(z[None], own, *got)


def coup_kernel(lists_ref, weights_ref, start_ref, sym_ref, left_ref, right_ref, o_ref, ext_ref):
    j_n = sym_ref.shape[0]
    ext_ref[0:REACH] = left_ref[...]
    ext_ref[REACH : REACH + j_n] = sym_ref[...]
    ext_ref[REACH + j_n :] = right_ref[...]
    t_n, _, r_n, s_n, _, _ = o_ref.shape
    start = start_ref[0]

    def tile(t, carry):
        for j in range(j_n):
            gj = start + j
            p0 = lists_ref[gj, 0] - start + REACH
            p1 = lists_ref[gj, 1] - start + REACH
            w0 = weights_ref[gj, 0]
            w1 = weights_ref[gj, 1]
            for r in range(r_n):
                i = t * r_n + r
                row = weights_ref[i, 0] * sym_ref[j, lists_ref[i, 0]].astype(jnp.float32)
                row = row + weights_ref[i, 1] * sym_ref[j, lists_ref[i, 1]].astype(jnp.float32)
                col = w0 * ext_ref[p0, i].astype(jnp.float32)
                col = col + w1 * ext_ref[p1, i].astype(jnp.float32)
                total = row.astype(jnp.bfloat16).astype(jnp.float32) + col.astype(
                    jnp.bfloat16
                ).astype(jnp.float32)
                o_ref[t, j // s_n, r, j % s_n] = total.astype(jnp.bfloat16)
        return carry

    lax.fori_loop(0, t_n, tile, 0)


def couple(lists, weights, start, sym, left, right, r_n, s_n):
    j_n, i_n, sr, sl = sym.shape
    return pl.pallas_call(
        coup_kernel,
        in_specs=[SMEM, SMEM, SMEM, VMEM, VMEM, VMEM],
        out_specs=VMEM,
        out_shape=jax.ShapeDtypeStruct((i_n // r_n, j_n // s_n, r_n, s_n, sr, sl), jnp.bfloat16),
        scratch_shapes=[pltpu.VMEM((j_n + 2 * REACH, i_n, sr, sl), jnp.bfloat16)],
        name="couple",
    )(lists, weights, start, sym, left, right)


def _dot(x, y):
    return jnp.dot(x, y, preferred_element_type=jnp.float32)


def pre_kernel(amp_ref, exch_ref, fock_ref, over_ref, o_ref):
    fock = fock_ref[...]
    over = over_ref[...]
    for s in range(amp_ref.shape[1]):
        amp = amp_ref[0, s]
        first = _dot(_dot(fock, amp).astype(jnp.bfloat16), over)
        second = _dot(_dot(over, amp).astype(jnp.bfloat16), fock)
        o_ref[0, s] = exch_ref[0, s].astype(jnp.float32) + first + second


def precompute(amp, exch, fock, over):
    rows, cols, w, _ = amp.shape
    big = pl.BlockSpec((1, cols, w, w), lambda k: (k, 0, 0, 0))
    mat = pl.BlockSpec((w, w), lambda k: (0, 0))
    return pl.pallas_call(
        pre_kernel,
        grid=(rows,),
        in_specs=[big, big, mat, mat],
        out_specs=big,
        out_shape=jax.ShapeDtypeStruct(amp.shape, jnp.float32),
        name="precompute",
    )(amp, exch, fock, over)


def post_kernel(
    occ_ref,
    base_ref,
    amp_ref,
    mask_i_ref,
    mask_j_ref,
    over_ref,
    trans_ref,
    tt_ref,
    energy_ref,
    *refs,
):
    coup_refs, (res_ref, new_ref) = refs[:-2], refs[-2:]
    k = pl.program_id(0)
    step, cols, w, _ = amp_ref.shape
    rows = pl.num_programs(0) * step
    over = over_ref[...]
    trans = trans_ref[...]
    tt = tt_ref[...]
    pairs = [(r, s) for r in range(step) for s in range(cols)]
    bf = lambda xs: [x.astype(jnp.bfloat16) for x in xs]

    def left(m, xs):
        return [_dot(m, x) for x in xs]

    def right(xs, m):
        return [_dot(x, m) for x in xs]

    two = []
    cm = []
    for r, s in pairs:
        row = jnp.maximum(mask_i_ref[r], mask_j_ref[s])
        two.append(row.T * row)
        coup = [c_ref[:, r, s].astype(jnp.float32).reshape(w, -1) for c_ref in coup_refs]
        cm.append(jnp.concatenate(coup, axis=1) * two[-1])
    third = right(bf(left(over, bf(cm))), over)
    res = [m * (base_ref[r, s] - t) for m, t, (r, s) in zip(two, third, pairs)]
    for x, (r, s) in zip(res, pairs):
        res_ref[r, s] = x
    q = right(bf(left(tt, bf(res))), trans)
    energy = energy_ref[...].T + energy_ref[...]
    z = [
        x / (energy - (occ_ref[k * step + r] + occ_ref[rows + s])) for x, (r, s) in zip(q, pairs)
    ]
    u = right(bf(left(trans, bf(z))), tt)
    for x, (r, s) in zip(u, pairs):
        new_ref[r, s] = (amp_ref[r, s].astype(jnp.float32) - x).astype(jnp.bfloat16)


def finish(occ, base, amp, coup, mask_i, mask_j, over, trans, energy):
    rows, cols, w, _ = amp.shape
    n, _, _, sr, sl = coup[0].shape
    step = 2
    big = pl.BlockSpec((step, cols, w, w), lambda k, *_: (k, 0, 0, 0))
    mat = pl.BlockSpec((w, w), lambda k, *_: (0, 0))
    return pl.pallas_call(
        post_kernel,
        grid_spec=pltpu.PrefetchScalarGridSpec(
            num_scalar_prefetch=1,
            grid=(rows // step,),
            in_specs=[
                big,
                big,
                pl.BlockSpec((step, 1, w), lambda k, *_: (k, 0, 0)),
                pl.BlockSpec((cols, 1, w), lambda k, *_: (0, 0, 0)),
                mat,
                mat,
                mat,
                pl.BlockSpec((1, w), lambda k, *_: (0, 0)),
            ]
            + [pl.BlockSpec((n, step, cols, sr, sl), lambda k, *_: (0, k, 0, 0, 0))] * len(coup),
            out_specs=[big, big],
        ),
        out_shape=[
            jax.ShapeDtypeStruct(amp.shape, jnp.float32),
            jax.ShapeDtypeStruct(amp.shape, jnp.bfloat16),
        ],
        name="finish",
    )(
        occ,
        base,
        amp,
        mask_i[:, None, :],
        mask_j[:, None, :],
        over,
        trans,
        trans.T,
        energy[None, :],
        *coup,
    )


def per_device(
    amplitudes,
    exchange,
    fock_virt,
    intersection,
    transform,
    virt_energy,
    occ_energy,
    partners,
    coupling,
    domain,
):
    rows, cols, width, _ = amplitudes.shape
    blocks = domain.shape[1]
    a_n = lax.axis_size("a")
    z_n = lax.axis_size("z")
    g_n = lax.axis_size("g")
    start_i = lax.axis_index("a") * rows
    start_z = lax.axis_index("z") * (g_n * cols)
    start_j = start_z + lax.axis_index("g") * cols
    plane = ("a", "g")
    n = a_n * g_n

    over = (jnp.eye(width, dtype=jnp.float32) + intersection.astype(jnp.float32)).astype(
        jnp.bfloat16
    )
    shape = (a_n, g_n, rows, cols, width // n, width // CHUNKS)
    z = lax.axis_index("z")

    def spread(x):
        return lax.all_to_all(x, plane, 0, 0, tiled=True)

    flipped = pack(amplitudes, n, True)
    own = pack(amplitudes, n, False)
    got = []
    last = None
    for h in range(CHUNKS):
        part = flipped[h]
        if h:
            part, last = lax.optimization_barrier((part, last))
        part = spread(part).reshape(shape)
        tiles = []
        for k in range(z_n):
            tile = lax.dynamic_index_in_dim(part, lax.rem(z + k, z_n), 0, keepdims=False)
            if k:
                tile = lax.ppermute(tile, "z", [(q, (q + k) % z_n) for q in range(z_n)])
            else:
                last = tile
            tiles.append(tile)
        got.append(tiles)
    up = [(k, k + 1) for k in range(z_n - 1)]
    down = [(k + 1, k) for k in range(z_n - 1)]
    base = precompute(amplitudes, exchange, fock_virt, over)
    coup = []
    for h in range(CHUNKS):
        part, last = lax.optimization_barrier((own[h], last))
        part = spread(part).reshape(shape)
        last = part
        sym, low, high = symmetrize(z, part, got[h])
        left = lax.ppermute(high, "z", up)
        right = lax.ppermute(low, "z", down)
        part = couple(partners, coupling, start_z[None], sym, left, right, rows, cols)
        coup.append(spread(part.reshape(own[h].shape)))

    masks = jnp.repeat(domain.astype(jnp.float32), width // blocks, axis=1)
    mask_i = lax.dynamic_slice_in_dim(masks, start_i, rows, 0)
    mask_j = lax.dynamic_slice_in_dim(masks, start_j, cols, 0)
    occ = jnp.concatenate(
        [
            lax.dynamic_slice_in_dim(occ_energy, start_i, rows, 0),
            lax.dynamic_slice_in_dim(occ_energy, start_j, cols, 0),
        ]
    )
    return tuple(
        finish(occ, base, amplitudes, coup, mask_i, mask_j, over, transform, virt_energy)
    )


def solution(mesh):
    i_n, j_n = mesh.shape["occi"], mesh.shape["occj"]
    group = j_n // i_n
    z_n = j_n // group
    inner = Mesh(mesh.devices.reshape(i_n, z_n, group), ("a", "z", "g"))
    pairs = P("a", ("z", "g"), None, None)
    return jax.shard_map(
        per_device,
        mesh=inner,
        in_specs=(pairs, pairs, P(), P(), P(), P(), P(), P(), P(), P()),
        out_specs=(pairs, pairs),
        check_vma=False,
    )
```

```python
import functools

import jax
import jax.numpy as jnp
from jax import lax
from jax.experimental import pallas as pl
from jax.experimental.pallas import tpu as pltpu
from jax.sharding import Mesh
from jax.sharding import PartitionSpec as P

REACH = 2
VMEM = pl.BlockSpec(memory_space=pltpu.VMEM)
SMEM = pl.BlockSpec(memory_space=pltpu.SMEM)


def pack_kernel(x_ref, o_ref, *, flip):
    n, _, _, sr, _ = o_ref.shape
    for r in range(x_ref.shape[0]):
        for s in range(x_ref.shape[1]):
            block = x_ref[r, s].astype(jnp.float32)
            if flip:
                block = block.T
            for u in range(n):
                o_ref[u, r, s] = block[sr * u : sr * u + sr].astype(jnp.bfloat16)


def pack(x, n, flip):
    rows, cols, w, _ = x.shape
    sr = w // n
    step = 2
    return pl.pallas_call(
        functools.partial(pack_kernel, flip=flip),
        grid=(rows // step,),
        in_specs=[pl.BlockSpec((step, cols, w, w), lambda k: (k, 0, 0, 0))],
        out_specs=pl.BlockSpec((n, step, cols, sr, w), lambda k: (0, k, 0, 0, 0)),
        out_shape=jax.ShapeDtypeStruct((n, rows, cols, sr, w), jnp.bfloat16),
        name="pack_flip" if flip else "pack",
    )(x)


def sym_kernel(z_ref, a_ref, *refs, split):
    got, (o_ref, lo_ref, hi_ref) = refs[:-3], refs[-3:]
    t_n, g_n, r_n, s_n, _, _ = a_ref.shape
    j_n = g_n * s_n
    at = 0
    for k, parts in enumerate(split):
        tile = got[at : at + parts]
        at += parts
        t = lax.rem(z_ref[0] + (t_n - k), t_n)
        for j in range(j_n):
            for i in range(r_n):
                own = a_ref[t, j // s_n, i, j % s_n].astype(jnp.float32)
                g = i // s_n
                b_ref = tile[g * parts // g_n]
                mir = b_ref[g % (g_n // parts), j, i % s_n].astype(jnp.float32)
                val = (0.5 * (own + mir)).astype(jnp.bfloat16)
                o_ref[j, t * r_n + i] = val
                if j < REACH:
                    lo_ref[j, t * r_n + i] = val
                if j >= j_n - REACH:
                    hi_ref[j - j_n + REACH, t * r_n + i] = val


def symmetrize(z, own, got):
    t_n, g_n, r_n, s_n, sr, sl = own.shape
    shape = lambda n: jax.ShapeDtypeStruct((n, t_n * r_n, sr, sl), jnp.bfloat16)
    flat = [part for tile in got for part in tile]
    return pl.pallas_call(
        functools.partial(sym_kernel, split=[len(tile) for tile in got]),
        in_specs=[SMEM, VMEM] + [VMEM] * len(flat),
        out_specs=[VMEM] * 3,
        out_shape=[shape(g_n * s_n), shape(REACH), shape(REACH)],
        name="sym",
    )(z[None], own, *flat)


def _couple_pair(lists_ref, weights_ref, row_of, col_of, gj, i):
    row = weights_ref[i, 0] * row_of(lists_ref[i, 0]).astype(jnp.float32)
    row = row + weights_ref[i, 1] * row_of(lists_ref[i, 1]).astype(jnp.float32)
    col = weights_ref[gj, 0] * col_of(lists_ref[gj, 0]).astype(jnp.float32)
    col = col + weights_ref[gj, 1] * col_of(lists_ref[gj, 1]).astype(jnp.float32)
    total = row.astype(jnp.bfloat16).astype(jnp.float32) + col.astype(jnp.bfloat16).astype(
        jnp.float32
    )
    return total.astype(jnp.bfloat16)


def inner_kernel(lists_ref, weights_ref, start_ref, sym_ref, o_ref):
    t_n, _, r_n, s_n, _, _ = o_ref.shape
    start = start_ref[0]
    first = (pl.program_id(0) + REACH // s_n) * s_n

    def tile(t, carry):
        for s in range(s_n):
            j = first + s
            for r in range(r_n):
                i = t * r_n + r
                o_ref[t, 0, r, s] = _couple_pair(
                    lists_ref,
                    weights_ref,
                    lambda p: sym_ref[j, p],
                    lambda p: sym_ref[p - start, i],
                    start + j,
                    i,
                )
        return carry

    lax.fori_loop(0, t_n, tile, 0)


def edge_kernel(
    lists_ref, weights_ref, start_ref, sym_ref, left_ref, right_ref, _, o_ref, ext_ref
):
    t_n, _, r_n, s_n, _, _ = o_ref.shape
    j_n = sym_ref.shape[0]
    per = REACH // s_n
    k = pl.program_id(0)
    start = start_ref[0]
    high = k >= per
    base = jnp.where(high, j_n - 2 * REACH, -REACH)
    j0 = jnp.where(high, j_n - REACH, 0) + lax.rem(k, per) * s_n

    @pl.when(k == 0)
    def _():
        ext_ref[0:REACH] = left_ref[...]
        ext_ref[REACH:] = sym_ref[0 : 2 * REACH]

    @pl.when(k == per)
    def _():
        ext_ref[0 : 2 * REACH] = sym_ref[j_n - 2 * REACH :]
        ext_ref[2 * REACH :] = right_ref[...]

    def tile(t, carry):
        for s in range(s_n):
            j = j0 + s
            for r in range(r_n):
                i = t * r_n + r
                o_ref[t, 0, r, s] = _couple_pair(
                    lists_ref,
                    weights_ref,
                    lambda p: sym_ref[j, p],
                    lambda p: ext_ref[p - start - base, i],
                    start + j,
                    i,
                )
        return carry

    lax.fori_loop(0, t_n, tile, 0)


def couple(lists, weights, start, sym, left, right, r_n, s_n):
    j_n, i_n, sr, sl = sym.shape
    t_n, g_n = i_n // r_n, j_n // s_n
    per = REACH // s_n
    out = jax.ShapeDtypeStruct((t_n, g_n, r_n, s_n, sr, sl), jnp.bfloat16)
    block = (t_n, 1, r_n, s_n, sr, sl)
    part = pl.pallas_call(
        inner_kernel,
        grid=(g_n - 2 * per,),
        in_specs=[SMEM, SMEM, SMEM, VMEM],
        out_specs=pl.BlockSpec(block, lambda k: (0, k + per, 0, 0, 0, 0)),
        out_shape=out,
        name="inner",
    )(lists, weights, start, sym)
    return pl.pallas_call(
        edge_kernel,
        grid=(2 * per,),
        in_specs=[SMEM, SMEM, SMEM, VMEM, VMEM, VMEM, pl.BlockSpec(memory_space=pl.ANY)],
        out_specs=pl.BlockSpec(
            block, lambda k: (0, k + jnp.where(k >= per, g_n - 2 * per, 0), 0, 0, 0, 0)
        ),
        out_shape=out,
        scratch_shapes=[pltpu.VMEM((3 * REACH, i_n, sr, sl), jnp.bfloat16)],
        input_output_aliases={6: 0},
        name="edge",
    )(lists, weights, start, sym, left, right, part)


def _dot(x, y):
    return jnp.dot(x, y, preferred_element_type=jnp.float32)


def pre_kernel(amp_ref, exch_ref, fock_ref, over_ref, o_ref):
    fock = fock_ref[...]
    over = over_ref[...]
    for s in range(amp_ref.shape[1]):
        amp = amp_ref[0, s]
        first = _dot(_dot(fock, amp).astype(jnp.bfloat16), over)
        second = _dot(_dot(over, amp).astype(jnp.bfloat16), fock)
        o_ref[0, s] = exch_ref[0, s].astype(jnp.float32) + first + second


def precompute(amp, exch, fock, over):
    rows, cols, w, _ = amp.shape
    big = pl.BlockSpec((1, cols, w, w), lambda k: (k, 0, 0, 0))
    mat = pl.BlockSpec((w, w), lambda k: (0, 0))
    return pl.pallas_call(
        pre_kernel,
        grid=(rows,),
        in_specs=[big, big, mat, mat],
        out_specs=big,
        out_shape=jax.ShapeDtypeStruct(amp.shape, jnp.float32),
        name="precompute",
    )(amp, exch, fock, over)


def post_kernel(
    occ_ref,
    base_ref,
    amp_ref,
    mask_i_ref,
    mask_j_ref,
    over_ref,
    trans_ref,
    tt_ref,
    energy_ref,
    coup_ref,
    res_ref,
    new_ref,
):
    k = pl.program_id(0)
    step, cols, w, _ = amp_ref.shape
    rows = pl.num_programs(0) * step
    over = over_ref[...]
    trans = trans_ref[...]
    tt = tt_ref[...]
    pairs = [(r, s) for r in range(step) for s in range(cols)]
    bf = lambda xs: [x.astype(jnp.bfloat16) for x in xs]

    def left(m, xs):
        return [_dot(m, x) for x in xs]

    def right(xs, m):
        return [_dot(x, m) for x in xs]

    two = []
    cm = []
    for r, s in pairs:
        row = jnp.maximum(mask_i_ref[r], mask_j_ref[s])
        two.append(row.T * row)
        coup = coup_ref[:, k * step + r, s].astype(jnp.float32).reshape(w, w)
        cm.append(coup * two[-1])
    third = right(bf(left(over, bf(cm))), over)
    res = [m * (base_ref[r, s] - t) for m, t, (r, s) in zip(two, third, pairs)]
    for x, (r, s) in zip(res, pairs):
        res_ref[r, s] = x
    q = right(bf(left(tt, bf(res))), trans)
    energy = energy_ref[...].T + energy_ref[...]
    z = [
        x / (energy - (occ_ref[k * step + r] + occ_ref[rows + s])) for x, (r, s) in zip(q, pairs)
    ]
    u = right(bf(left(trans, bf(z))), tt)
    for x, (r, s) in zip(u, pairs):
        new_ref[r, s] = (amp_ref[r, s].astype(jnp.float32) - x).astype(jnp.bfloat16)


def finish(occ, base, amp, coup, mask_i, mask_j, over, trans, energy):
    rows, cols, w, _ = amp.shape
    step = 2
    big = pl.BlockSpec((step, cols, w, w), lambda k, *_: (k, 0, 0, 0))
    mat = pl.BlockSpec((w, w), lambda k, *_: (0, 0))
    return pl.pallas_call(
        post_kernel,
        grid_spec=pltpu.PrefetchScalarGridSpec(
            num_scalar_prefetch=1,
            grid=(rows // step,),
            in_specs=[
                big,
                big,
                pl.BlockSpec((step, 1, w), lambda k, *_: (k, 0, 0)),
                pl.BlockSpec((cols, 1, w), lambda k, *_: (0, 0, 0)),
                mat,
                mat,
                mat,
                pl.BlockSpec((1, w), lambda k, *_: (0, 0)),
                VMEM,
            ],
            out_specs=[big, big],
        ),
        out_shape=[
            jax.ShapeDtypeStruct(amp.shape, jnp.float32),
            jax.ShapeDtypeStruct(amp.shape, jnp.bfloat16),
        ],
        name="finish",
    )(
        occ,
        base,
        amp,
        mask_i[:, None, :],
        mask_j[:, None, :],
        over,
        trans,
        trans.T,
        energy[None, :],
        coup,
    )


def per_device(
    amplitudes,
    exchange,
    fock_virt,
    intersection,
    transform,
    virt_energy,
    occ_energy,
    partners,
    coupling,
    domain,
):
    rows, cols, width, _ = amplitudes.shape
    blocks = domain.shape[1]
    a_n = lax.axis_size("a")
    z_n = lax.axis_size("z")
    g_n = lax.axis_size("g")
    start_i = lax.axis_index("a") * rows
    start_z = lax.axis_index("z") * (g_n * cols)
    start_j = start_z + lax.axis_index("g") * cols
    plane = ("a", "g")
    n = a_n * g_n

    over = (jnp.eye(width, dtype=jnp.float32) + intersection.astype(jnp.float32)).astype(
        jnp.bfloat16
    )
    shape = (a_n, g_n, rows, cols, width // n, width)
    z = lax.axis_index("z")

    def spread(x):
        return lax.all_to_all(x, plane, 0, 0, tiled=True)

    def shift(x, k):
        return lax.ppermute(x, "z", [(q, (q + k) % z_n) for q in range(z_n)])

    part = spread(pack(amplitudes, n, True)).reshape(shape)
    own = pack(amplitudes, n, False)
    tiles = [
        lax.dynamic_index_in_dim(part, lax.rem(z + k, z_n), 0, keepdims=False) for k in range(z_n)
    ]
    half = g_n // 2
    far = z_n // 2
    relay = shift(tiles[far][half:], z_n - 1)
    got = []
    for k in range(z_n):
        if k == 0:
            got.append([tiles[k]])
        elif k == far:
            got.append([shift(tiles[k][:half], k)])
        else:
            got.append([shift(tiles[k], k)])
    got[far].append(shift(relay, far + 1))
    base = precompute(amplitudes, exchange, fock_virt, over)
    own, _ = lax.optimization_barrier((own, tiles[0]))
    own = spread(own).reshape(shape)
    sym, low, high = symmetrize(z, own, got)
    left = lax.ppermute(high, "z", [(k, k + 1) for k in range(z_n - 1)])
    right = lax.ppermute(low, "z", [(k + 1, k) for k in range(z_n - 1)])
    part = couple(partners, coupling, start_z[None], sym, left, right, rows, cols)
    coup = spread(part.reshape(n, rows, cols, width // n, width))

    masks = jnp.repeat(domain.astype(jnp.float32), width // blocks, axis=1)
    mask_i = lax.dynamic_slice_in_dim(masks, start_i, rows, 0)
    mask_j = lax.dynamic_slice_in_dim(masks, start_j, cols, 0)
    occ = jnp.concatenate(
        [
            lax.dynamic_slice_in_dim(occ_energy, start_i, rows, 0),
            lax.dynamic_slice_in_dim(occ_energy, start_j, cols, 0),
        ]
    )
    return tuple(
        finish(occ, base, amplitudes, coup, mask_i, mask_j, over, transform, virt_energy)
    )


def solution(mesh):
    i_n, j_n = mesh.shape["occi"], mesh.shape["occj"]
    group = j_n // i_n
    z_n = j_n // group
    inner = Mesh(mesh.devices.reshape(i_n, z_n, group), ("a", "z", "g"))
    pairs = P("a", ("z", "g"), None, None)
    return jax.shard_map(
        per_device,
        mesh=inner,
        in_specs=(pairs, pairs, P(), P(), P(), P(), P(), P(), P(), P()),
        out_specs=(pairs, pairs),
        check_vma=False,
    )
```

```python
import functools

import jax
import jax.numpy as jnp
from jax import lax
from jax.experimental import pallas as pl
from jax.experimental.pallas import tpu as pltpu
from jax.sharding import Mesh
from jax.sharding import PartitionSpec as P

REACH = 2
VMEM = pl.BlockSpec(memory_space=pltpu.VMEM)
SMEM = pl.BlockSpec(memory_space=pltpu.SMEM)


def pack_kernel(x_ref, o_ref, *, flip):
    n, _, _, sr, _ = o_ref.shape
    for r in range(x_ref.shape[0]):
        for s in range(x_ref.shape[1]):
            block = x_ref[r, s].astype(jnp.float32)
            if flip:
                block = block.T
            for u in range(n):
                o_ref[u, r, s] = block[sr * u : sr * u + sr].astype(jnp.bfloat16)


def pack(x, n, flip):
    rows, cols, w, _ = x.shape
    sr = w // n
    step = 2
    return pl.pallas_call(
        functools.partial(pack_kernel, flip=flip),
        grid=(rows // step,),
        in_specs=[pl.BlockSpec((step, cols, w, w), lambda k: (k, 0, 0, 0))],
        out_specs=pl.BlockSpec((n, step, cols, sr, w), lambda k: (0, k, 0, 0, 0)),
        out_shape=jax.ShapeDtypeStruct((n, rows, cols, sr, w), jnp.bfloat16),
        name="pack_flip" if flip else "pack",
    )(x)


def _mirrored(got, split, k, j, i, g_n, s_n):
    at = sum(split[:k])
    parts = split[k]
    g = i // s_n
    return got[at + g * parts // g_n][g % (g_n // parts), j, i % s_n]


def _sym(own, mir):
    return (0.5 * (own.astype(jnp.float32) + mir.astype(jnp.float32))).astype(jnp.bfloat16)


def halo_kernel(z_ref, a_ref, *refs, split):
    got, (lo_ref, hi_ref) = refs[:-2], refs[-2:]
    t_n, g_n, r_n, s_n, _, _ = a_ref.shape
    j_n = g_n * s_n
    for k in range(t_n):
        t = lax.rem(z_ref[0] + (t_n - k), t_n)
        for o_ref, base in ((lo_ref, 0), (hi_ref, j_n - REACH)):
            for c in range(REACH):
                j = base + c
                for i in range(r_n):
                    mir = _mirrored(got, split, k, j, i, g_n, s_n)
                    o_ref[c, t * r_n + i] = _sym(a_ref[t, j // s_n, i, j % s_n], mir)


def _mix(weights_ref, at, x0, x1):
    total = weights_ref[0, at] * x0.astype(jnp.float32)
    return (total + weights_ref[1, at] * x1.astype(jnp.float32)).astype(jnp.bfloat16)


def inner_kernel(
    z_ref, lists_ref, weights_ref, start_ref, a_ref, lo_ref, hi_ref, *refs, split
):
    got, (mid_ref, o_ref, all_ref) = refs[:-3], refs[-3:]
    t_n, g_n, r_n, s_n, _, _ = a_ref.shape
    j_n = g_n * s_n
    start = start_ref[0]
    all_ref[0:REACH] = lo_ref[...]
    all_ref[j_n - REACH :] = hi_ref[...]
    for k in range(t_n):
        t = lax.rem(z_ref[0] + (t_n - k), t_n)
        for j in range(REACH, j_n - REACH):
            for i in range(r_n):
                mir = _mirrored(got, split, k, j, i, g_n, s_n)
                val = _sym(a_ref[t, j // s_n, i, j % s_n], mir)
                all_ref[j, t * r_n + i] = val
                mid_ref[j - REACH, t * r_n + i] = val

    def tile(t, carry):
        for j in range(j_n):
            gj = start + j
            for r in range(r_n):
                i = t * r_n + r
                out = _mix(weights_ref, i, all_ref[j, lists_ref[0, i]], all_ref[j, lists_ref[1, i]])
                if REACH <= j < j_n - REACH:
                    x0 = all_ref[lists_ref[0, gj] - start, i]
                    x1 = all_ref[lists_ref[1, gj] - start, i]
                    col = _mix(weights_ref, gj, x0, x1)
                    out = (out.astype(jnp.float32) + col.astype(jnp.float32)).astype(jnp.bfloat16)
                o_ref[t, j // s_n, r, j % s_n] = out
        return carry

    lax.fori_loop(0, t_n, tile, 0)


def edge_kernel(
    lists_ref, weights_ref, start_ref, left_ref, lo_ref, mid_ref, hi_ref, right_ref, x_ref, o_ref, ext_ref, sems
):
    t_n, _, r_n, s_n, _, _ = o_ref.shape
    k = pl.program_id(0)
    per = REACH // s_n
    start = start_ref[0]
    copies = []
    at = 0
    for ref, q0, n in (
        (left_ref, 0, REACH),
        (lo_ref, 0, REACH),
        (mid_ref, 0, REACH),
        (mid_ref, REACH, REACH),
        (hi_ref, 0, REACH),
        (right_ref, 0, REACH),
    ):
        src = ref.at[pl.ds(q0, n)]
        copies.append(pltpu.make_async_copy(src, ext_ref.at[pl.ds(at, n)], sems.at[len(copies)]))
        at += n

    @pl.when(k == 0)
    def _():
        for c in copies:
            c.start()
        for c in copies[:3]:
            c.wait()

    @pl.when(k == per)
    def _():
        for c in copies[3:]:
            c.wait()

    high = k >= per
    j0 = k * s_n
    gap = mid_ref.shape[0] - 2 * REACH
    gj0 = start + j0 + jnp.where(high, mid_ref.shape[0], 0)
    base = start - REACH + jnp.where(high, gap, 0)

    def tile(t, carry):
        for s in range(s_n):
            gj = gj0 + s
            for r in range(r_n):
                i = t * r_n + r
                col = _mix(
                    weights_ref,
                    gj,
                    ext_ref[lists_ref[0, gj] - base, i],
                    ext_ref[lists_ref[1, gj] - base, i],
                )
                row = x_ref[t, 0, r, s].astype(jnp.float32)
                o_ref[t, 0, r, s] = (row + col.astype(jnp.float32)).astype(jnp.bfloat16)
        return carry

    lax.fori_loop(0, t_n, tile, 0)


def halo_columns(z, own, got):
    t_n, _, r_n, _, sr, sl = own.shape
    split = [len(tile) for tile in got]
    flat = [part for tile in got for part in tile]
    return pl.pallas_call(
        functools.partial(halo_kernel, split=split),
        in_specs=[SMEM, VMEM] + [VMEM] * len(flat),
        out_specs=[VMEM] * 2,
        out_shape=[jax.ShapeDtypeStruct((REACH, t_n * r_n, sr, sl), jnp.bfloat16)] * 2,
        name="halo",
    )(z[None], own, *flat)


def couple_inner(z, lists, weights, start, own, got, low, high):
    t_n, g_n, r_n, s_n, sr, sl = own.shape
    j_n = g_n * s_n
    split = [len(tile) for tile in got]
    flat = [part for tile in got for part in tile]
    columns = lambda n: (n, t_n * r_n, sr, sl)
    return pl.pallas_call(
        functools.partial(inner_kernel, split=split),
        in_specs=[SMEM] * 4 + [VMEM] * (3 + len(flat)),
        out_specs=[VMEM] * 2,
        out_shape=[
            jax.ShapeDtypeStruct(columns(j_n - 2 * REACH), jnp.bfloat16),
            jax.ShapeDtypeStruct(own.shape, jnp.bfloat16),
        ],
        scratch_shapes=[pltpu.VMEM(columns(j_n), jnp.bfloat16)],
        name="inner",
    )(z[None], lists, weights, start, own, low, high, *flat)


def couple_edge(lists, weights, start, left, low, middle, high, right, part):
    t_n, g_n, r_n, s_n, sr, sl = part.shape
    per = REACH // s_n
    i_n = t_n * r_n
    hbm = pl.BlockSpec(memory_space=pl.ANY)
    block = pl.BlockSpec(
        (t_n, 1, r_n, s_n, sr, sl),
        lambda k: (0, k + jnp.where(k >= per, g_n - 2 * per, 0), 0, 0, 0, 0),
    )
    return pl.pallas_call(
        edge_kernel,
        grid=(2 * per,),
        in_specs=[SMEM, SMEM, SMEM] + [hbm] * 5 + [block],
        out_specs=block,
        out_shape=jax.ShapeDtypeStruct(part.shape, jnp.bfloat16),
        scratch_shapes=[
            pltpu.VMEM((6 * REACH, i_n, sr, sl), jnp.bfloat16),
            pltpu.SemaphoreType.DMA((6,)),
        ],
        input_output_aliases={8: 0},
        name="edge",
    )(lists, weights, start, left, low, middle, high, right, part)


def _dot(x, y):
    return jnp.dot(x, y, preferred_element_type=jnp.float32)


def pre_kernel(x_ref, amp_ref, left_ref, right_ref, o_ref):
    left = left_ref[...]
    right = right_ref[...]
    for s in range(amp_ref.shape[1]):
        term = _dot(_dot(left, amp_ref[0, s]).astype(jnp.bfloat16), right)
        o_ref[0, s] = x_ref[0, s].astype(jnp.float32) + term


def add_term(x, amp, left, right):
    rows, cols, w, _ = amp.shape
    big = pl.BlockSpec((1, cols, w, w), lambda k: (k, 0, 0, 0))
    mat = pl.BlockSpec((w, w), lambda k: (0, 0))
    return pl.pallas_call(
        pre_kernel,
        grid=(rows,),
        in_specs=[big, big, mat, mat],
        out_specs=big,
        out_shape=jax.ShapeDtypeStruct(amp.shape, jnp.float32),
        name="term",
    )(x, amp, left, right)


def post_kernel(
    occ_ref,
    base_ref,
    amp_ref,
    mask_i_ref,
    mask_j_ref,
    over_ref,
    trans_ref,
    tt_ref,
    energy_ref,
    coup_ref,
    res_ref,
    new_ref,
):
    k = pl.program_id(0)
    step, cols, w, _ = amp_ref.shape
    rows = pl.num_programs(0) * step
    over = over_ref[...]
    trans = trans_ref[...]
    tt = tt_ref[...]
    pairs = [(r, s) for r in range(step) for s in range(cols)]
    bf = lambda xs: [x.astype(jnp.bfloat16) for x in xs]

    def left(m, xs):
        return [_dot(m, x) for x in xs]

    def right(xs, m):
        return [_dot(x, m) for x in xs]

    two = []
    cm = []
    for r, s in pairs:
        row = jnp.maximum(mask_i_ref[r], mask_j_ref[s])
        two.append(row.T * row)
        coup = coup_ref[:, r, s].astype(jnp.float32).reshape(w, w)
        cm.append(coup * two[-1])
    third = right(bf(left(over, bf(cm))), over)
    res = [m * (base_ref[r, s] - t) for m, t, (r, s) in zip(two, third, pairs)]
    for x, (r, s) in zip(res, pairs):
        res_ref[r, s] = x
    q = right(bf(left(tt, bf(res))), trans)
    energy = energy_ref[...].T + energy_ref[...]
    z = [
        x / (energy - (occ_ref[k * step + r] + occ_ref[rows + s])) for x, (r, s) in zip(q, pairs)
    ]
    u = right(bf(left(trans, bf(z))), tt)
    for x, (r, s) in zip(u, pairs):
        new_ref[r, s] = (amp_ref[r, s].astype(jnp.float32) - x).astype(jnp.bfloat16)


def finish(occ, base, amp, coup, mask_i, mask_j, over, trans, energy):
    rows, cols, w, _ = amp.shape
    n, _, _, sr, _ = coup.shape
    step = 2
    big = pl.BlockSpec((step, cols, w, w), lambda k, *_: (k, 0, 0, 0))
    mat = pl.BlockSpec((w, w), lambda k, *_: (0, 0))
    return pl.pallas_call(
        post_kernel,
        grid_spec=pltpu.PrefetchScalarGridSpec(
            num_scalar_prefetch=1,
            grid=(rows // step,),
            in_specs=[
                big,
                big,
                pl.BlockSpec((step, 1, w), lambda k, *_: (k, 0, 0)),
                pl.BlockSpec((cols, 1, w), lambda k, *_: (0, 0, 0)),
                mat,
                mat,
                mat,
                pl.BlockSpec((1, w), lambda k, *_: (0, 0)),
                pl.BlockSpec((n, step, cols, sr, w), lambda k, *_: (0, k, 0, 0, 0)),
            ],
            out_specs=[big, big],
        ),
        out_shape=[
            jax.ShapeDtypeStruct(amp.shape, jnp.float32),
            jax.ShapeDtypeStruct(amp.shape, jnp.bfloat16),
        ],
        name="finish",
    )(
        occ,
        base,
        amp,
        mask_i[:, None, :],
        mask_j[:, None, :],
        over,
        trans,
        trans.T,
        energy[None, :],
        coup,
    )


def per_device(
    amplitudes,
    exchange,
    fock_virt,
    intersection,
    transform,
    virt_energy,
    occ_energy,
    partners,
    coupling,
    domain,
):
    rows, cols, width, _ = amplitudes.shape
    blocks = domain.shape[1]
    a_n = lax.axis_size("a")
    z_n = lax.axis_size("z")
    g_n = lax.axis_size("g")
    start_i = lax.axis_index("a") * rows
    start_z = lax.axis_index("z") * (g_n * cols)
    start_j = start_z + lax.axis_index("g") * cols
    plane = ("a", "g")
    n = a_n * g_n

    over = (jnp.eye(width, dtype=jnp.float32) + intersection.astype(jnp.float32)).astype(
        jnp.bfloat16
    )
    shape = (a_n, g_n, rows, cols, width // n, width)
    z = lax.axis_index("z")

    def spread(x):
        return lax.all_to_all(x, plane, 0, 0, tiled=True)

    def shift(x, k):
        return lax.ppermute(x, "z", [(q, (q + k) % z_n) for q in range(z_n)])

    part = spread(pack(amplitudes, n, True)).reshape(shape)
    own = pack(amplitudes, n, False)
    tiles = [
        lax.dynamic_index_in_dim(part, lax.rem(z + k, z_n), 0, keepdims=False) for k in range(z_n)
    ]
    half = g_n // 2
    far = z_n // 2
    relay = shift(tiles[far][half:], far + 1)
    got = []
    for k in range(z_n):
        if k == 0:
            got.append([tiles[k]])
        elif k == far:
            got.append([shift(tiles[k][:half], k)])
        else:
            got.append([shift(tiles[k], k)])
    got[far].append(shift(relay, z_n - 1))
    base = add_term(exchange, amplitudes, fock_virt, over)
    base = add_term(base, amplitudes, over, fock_virt)
    own, _ = lax.optimization_barrier((own, tiles[0]))
    own = spread(own).reshape(shape)
    low, high = halo_columns(z, own, got)
    left = lax.ppermute(high, "z", [(k, k + 1) for k in range(z_n - 1)])
    right = lax.ppermute(low, "z", [(k + 1, k) for k in range(z_n - 1)])
    lists = partners.T
    weights = coupling.T
    middle, part = couple_inner(z, lists, weights, start_z[None], own, got, low, high)
    part = couple_edge(lists, weights, start_z[None], left, low, middle, high, right, part)
    coup = spread(part.reshape(n, rows, cols, width // n, width))

    masks = jnp.repeat(domain.astype(jnp.float32), width // blocks, axis=1)
    mask_i = lax.dynamic_slice_in_dim(masks, start_i, rows, 0)
    mask_j = lax.dynamic_slice_in_dim(masks, start_j, cols, 0)
    occ = jnp.concatenate(
        [
            lax.dynamic_slice_in_dim(occ_energy, start_i, rows, 0),
            lax.dynamic_slice_in_dim(occ_energy, start_j, cols, 0),
        ]
    )
    return tuple(
        finish(occ, base, amplitudes, coup, mask_i, mask_j, over, transform, virt_energy)
    )


def solution(mesh):
    i_n, j_n = mesh.shape["occi"], mesh.shape["occj"]
    group = j_n // i_n
    z_n = j_n // group
    inner = Mesh(mesh.devices.reshape(i_n, z_n, group), ("a", "z", "g"))
    pairs = P("a", ("z", "g"), None, None)
    return jax.shard_map(
        per_device,
        mesh=inner,
        in_specs=(pairs, pairs, P(), P(), P(), P(), P(), P(), P(), P()),
        out_specs=(pairs, pairs),
        check_vma=False,
    )
```

```python
import functools

import jax
import jax.numpy as jnp
from jax import lax
from jax.experimental import pallas as pl
from jax.experimental.pallas import tpu as pltpu
from jax.sharding import Mesh
from jax.sharding import PartitionSpec as P

REACH = 2
VMEM = pl.BlockSpec(memory_space=pltpu.VMEM)
SMEM = pl.BlockSpec(memory_space=pltpu.SMEM)


def near(x):
    return pltpu.with_memory_space_constraint(x, pltpu.VMEM)


def pack_kernel(x_ref, o_ref, *, flip):
    n, _, _, sr, w = o_ref.shape
    for r in range(x_ref.shape[0]):
        for s in range(x_ref.shape[1]):
            block = x_ref[r, s]
            if flip:
                block = block.T
            o_ref[:, r, s] = block.reshape(n, sr, w)


def pack(x, n, flip):
    rows, cols, w, _ = x.shape
    sr = w // n
    step = 4
    return pl.pallas_call(
        functools.partial(pack_kernel, flip=flip),
        grid=(rows // step,),
        in_specs=[pl.BlockSpec((step, cols, w, w), lambda k: (k, 0, 0, 0))],
        out_specs=pl.BlockSpec((n, step, cols, sr, w), lambda k: (0, k, 0, 0, 0)),
        out_shape=jax.ShapeDtypeStruct((n, rows, cols, sr, w), jnp.bfloat16),
        name="pack_flip" if flip else "pack",
    )(x)


def _mirrored(got, split, k, j, i, g_n, s_n):
    at = sum(split[:k])
    parts = split[k]
    g = i // s_n
    return got[at + g * parts // g_n][g % (g_n // parts), j, i % s_n]


def _sym(own, mir):
    return (0.5 * (own.astype(jnp.float32) + mir.astype(jnp.float32))).astype(jnp.bfloat16)


def halo_kernel(z_ref, a_ref, *refs, split):
    got, (lo_ref, hi_ref) = refs[:-2], refs[-2:]
    t_n, g_n, r_n, s_n, _, _ = a_ref.shape
    j_n = g_n * s_n
    for k in range(t_n):
        t = lax.rem(z_ref[0] + (t_n - k), t_n)
        for o_ref, base in ((lo_ref, 0), (hi_ref, j_n - REACH)):
            for c in range(REACH):
                j = base + c
                for i in range(r_n):
                    mir = _mirrored(got, split, k, j, i, g_n, s_n)
                    o_ref[c, t * r_n + i] = _sym(a_ref[t, j // s_n, i, j % s_n], mir)


def _mix(weights_ref, at, x0, x1):
    total = weights_ref[0, at] * x0.astype(jnp.float32)
    return (total + weights_ref[1, at] * x1.astype(jnp.float32)).astype(jnp.bfloat16)


def inner_kernel(
    z_ref, lists_ref, weights_ref, start_ref, a_ref, lo_ref, hi_ref, *refs, split
):
    got, (mid_ref, o_ref, all_ref) = refs[:-3], refs[-3:]
    t_n, g_n, r_n, s_n, _, _ = a_ref.shape
    j_n = g_n * s_n
    start = start_ref[0]
    all_ref[0:REACH] = lo_ref[...]
    all_ref[j_n - REACH :] = hi_ref[...]
    for k in range(t_n):
        t = lax.rem(z_ref[0] + (t_n - k), t_n)
        for j in range(REACH, j_n - REACH):
            for i in range(r_n):
                mir = _mirrored(got, split, k, j, i, g_n, s_n)
                val = _sym(a_ref[t, j // s_n, i, j % s_n], mir)
                all_ref[j, t * r_n + i] = val
                mid_ref[j - REACH, t * r_n + i] = val

    def tile(t, carry):
        for j in range(j_n):
            gj = start + j
            for r in range(r_n):
                i = t * r_n + r
                out = _mix(weights_ref, i, all_ref[j, lists_ref[0, i]], all_ref[j, lists_ref[1, i]])
                if REACH <= j < j_n - REACH:
                    x0 = all_ref[lists_ref[0, gj] - start, i]
                    x1 = all_ref[lists_ref[1, gj] - start, i]
                    col = _mix(weights_ref, gj, x0, x1)
                    out = (out.astype(jnp.float32) + col.astype(jnp.float32)).astype(jnp.bfloat16)
                o_ref[t, j // s_n, r, j % s_n] = out
        return carry

    lax.fori_loop(0, t_n, tile, 0)


def edge_kernel(
    lists_ref, weights_ref, start_ref, left_ref, lo_ref, mid_ref, hi_ref, right_ref, x_ref, o_ref, ext_ref, sems
):
    t_n, _, r_n, s_n, _, _ = o_ref.shape
    k = pl.program_id(0)
    per = REACH // s_n
    start = start_ref[0]
    copies = []
    at = 0
    for ref, q0, n in (
        (left_ref, 0, REACH),
        (lo_ref, 0, REACH),
        (mid_ref, 0, REACH),
        (mid_ref, REACH, REACH),
        (hi_ref, 0, REACH),
        (right_ref, 0, REACH),
    ):
        src = ref.at[pl.ds(q0, n)]
        copies.append(pltpu.make_async_copy(src, ext_ref.at[pl.ds(at, n)], sems.at[len(copies)]))
        at += n

    @pl.when(k == 0)
    def _():
        for c in copies:
            c.start()
        for c in copies[:3]:
            c.wait()

    @pl.when(k == per)
    def _():
        for c in copies[3:]:
            c.wait()

    high = k >= per
    j0 = k * s_n
    gap = mid_ref.shape[0] - 2 * REACH
    gj0 = start + j0 + jnp.where(high, mid_ref.shape[0], 0)
    base = start - REACH + jnp.where(high, gap, 0)

    def tile(t, carry):
        for s in range(s_n):
            gj = gj0 + s
            for r in range(r_n):
                i = t * r_n + r
                col = _mix(
                    weights_ref,
                    gj,
                    ext_ref[lists_ref[0, gj] - base, i],
                    ext_ref[lists_ref[1, gj] - base, i],
                )
                row = x_ref[t, 0, r, s].astype(jnp.float32)
                o_ref[t, 0, r, s] = (row + col.astype(jnp.float32)).astype(jnp.bfloat16)
        return carry

    lax.fori_loop(0, t_n, tile, 0)


def halo_columns(z, own, got):
    t_n, _, r_n, _, sr, sl = own.shape
    split = [len(tile) for tile in got]
    flat = [part for tile in got for part in tile]
    return pl.pallas_call(
        functools.partial(halo_kernel, split=split),
        in_specs=[SMEM, VMEM] + [VMEM] * len(flat),
        out_specs=[VMEM] * 2,
        out_shape=[jax.ShapeDtypeStruct((REACH, t_n * r_n, sr, sl), jnp.bfloat16)] * 2,
        name="halo",
    )(z[None], own, *flat)


def couple_inner(z, lists, weights, start, own, got, low, high):
    t_n, g_n, r_n, s_n, sr, sl = own.shape
    j_n = g_n * s_n
    split = [len(tile) for tile in got]
    flat = [part for tile in got for part in tile]
    columns = lambda n: (n, t_n * r_n, sr, sl)
    return pl.pallas_call(
        functools.partial(inner_kernel, split=split),
        in_specs=[SMEM] * 4 + [VMEM] * (3 + len(flat)),
        out_specs=[VMEM] * 2,
        out_shape=[
            jax.ShapeDtypeStruct(columns(j_n - 2 * REACH), jnp.bfloat16),
            jax.ShapeDtypeStruct(own.shape, jnp.bfloat16),
        ],
        scratch_shapes=[pltpu.VMEM(columns(j_n), jnp.bfloat16)],
        name="inner",
    )(z[None], lists, weights, start, own, low, high, *flat)


def couple_edge(lists, weights, start, left, low, middle, high, right, part):
    t_n, g_n, r_n, s_n, sr, sl = part.shape
    per = REACH // s_n
    i_n = t_n * r_n
    hbm = pl.BlockSpec(memory_space=pl.ANY)
    block = pl.BlockSpec(
        (t_n, 1, r_n, s_n, sr, sl),
        lambda k: (0, k + jnp.where(k >= per, g_n - 2 * per, 0), 0, 0, 0, 0),
    )
    return pl.pallas_call(
        edge_kernel,
        grid=(2 * per,),
        in_specs=[SMEM, SMEM, SMEM, VMEM, hbm, hbm, hbm, VMEM, block],
        out_specs=block,
        out_shape=jax.ShapeDtypeStruct(part.shape, jnp.bfloat16),
        scratch_shapes=[
            pltpu.VMEM((6 * REACH, i_n, sr, sl), jnp.bfloat16),
            pltpu.SemaphoreType.DMA((6,)),
        ],
        input_output_aliases={8: 0},
        name="edge",
    )(lists, weights, start, left, low, middle, high, right, part)


def _dot(x, y):
    return jnp.dot(x, y, preferred_element_type=jnp.float32)


def pre_kernel(x_ref, amp_ref, left_ref, right_ref, o_ref):
    left = left_ref[...]
    right = right_ref[...]
    for s in range(amp_ref.shape[1]):
        term = _dot(_dot(left, amp_ref[0, s]).astype(jnp.bfloat16), right)
        o_ref[0, s] = x_ref[0, s].astype(jnp.float32) + term


def add_term(x, amp, left, right):
    rows, cols, w, _ = amp.shape
    big = pl.BlockSpec((1, cols, w, w), lambda k: (k, 0, 0, 0))
    mat = pl.BlockSpec((w, w), lambda k: (0, 0))
    return pl.pallas_call(
        pre_kernel,
        grid=(rows,),
        in_specs=[big, big, mat, mat],
        out_specs=big,
        out_shape=jax.ShapeDtypeStruct(amp.shape, jnp.float32),
        name="term",
    )(x, amp, left, right)


def post_kernel(
    occ_ref,
    base_ref,
    amp_ref,
    mask_i_ref,
    mask_j_ref,
    over_ref,
    trans_ref,
    tt_ref,
    energy_ref,
    coup_ref,
    res_ref,
    new_ref,
):
    k = pl.program_id(0)
    step, cols, w, _ = amp_ref.shape
    rows = pl.num_programs(0) * step
    over = over_ref[...]
    trans = trans_ref[...]
    tt = tt_ref[...]
    pairs = [(r, s) for r in range(step) for s in range(cols)]
    bf = lambda xs: [x.astype(jnp.bfloat16) for x in xs]

    def left(m, xs):
        return [_dot(m, x) for x in xs]

    def right(xs, m):
        return [_dot(x, m) for x in xs]

    two = []
    cm = []
    for r, s in pairs:
        row = jnp.maximum(mask_i_ref[r], mask_j_ref[s])
        two.append(row.T * row)
        coup = coup_ref[:, k * step + r, s].astype(jnp.float32).reshape(w, w)
        cm.append(coup * two[-1])
    third = right(bf(left(over, bf(cm))), over)
    res = [m * (base_ref[r, s] - t) for m, t, (r, s) in zip(two, third, pairs)]
    for x, (r, s) in zip(res, pairs):
        res_ref[r, s] = x
    q = right(bf(left(tt, bf(res))), trans)
    energy = energy_ref[...].T + energy_ref[...]
    z = [
        x / (energy - (occ_ref[k * step + r] + occ_ref[rows + s])) for x, (r, s) in zip(q, pairs)
    ]
    u = right(bf(left(trans, bf(z))), tt)
    for x, (r, s) in zip(u, pairs):
        new_ref[r, s] = (amp_ref[r, s].astype(jnp.float32) - x).astype(jnp.bfloat16)


def finish(occ, base, amp, coup, mask_i, mask_j, over, trans, energy):
    rows, cols, w, _ = amp.shape
    step = 2
    big = pl.BlockSpec((step, cols, w, w), lambda k, *_: (k, 0, 0, 0))
    mat = pl.BlockSpec((w, w), lambda k, *_: (0, 0))
    return pl.pallas_call(
        post_kernel,
        grid_spec=pltpu.PrefetchScalarGridSpec(
            num_scalar_prefetch=1,
            grid=(rows // step,),
            in_specs=[
                big,
                big,
                pl.BlockSpec((step, 1, w), lambda k, *_: (k, 0, 0)),
                pl.BlockSpec((cols, 1, w), lambda k, *_: (0, 0, 0)),
                mat,
                mat,
                mat,
                pl.BlockSpec((1, w), lambda k, *_: (0, 0)),
                VMEM,
            ],
            out_specs=[big, big],
        ),
        out_shape=[
            jax.ShapeDtypeStruct(amp.shape, jnp.float32),
            jax.ShapeDtypeStruct(amp.shape, jnp.bfloat16),
        ],
        name="finish",
    )(
        occ,
        base,
        amp,
        mask_i[:, None, :],
        mask_j[:, None, :],
        over,
        trans,
        trans.T,
        energy[None, :],
        coup,
    )


def per_device(
    amplitudes,
    exchange,
    fock_virt,
    intersection,
    transform,
    virt_energy,
    occ_energy,
    partners,
    coupling,
    domain,
):
    rows, cols, width, _ = amplitudes.shape
    blocks = domain.shape[1]
    a_n = lax.axis_size("a")
    z_n = lax.axis_size("z")
    g_n = lax.axis_size("g")
    start_i = lax.axis_index("a") * rows
    start_z = lax.axis_index("z") * (g_n * cols)
    start_j = start_z + lax.axis_index("g") * cols
    plane = ("a", "g")
    n = a_n * g_n

    over = (jnp.eye(width, dtype=jnp.float32) + intersection.astype(jnp.float32)).astype(
        jnp.bfloat16
    )
    shape = (a_n, g_n, rows, cols, width // n, width)
    z = lax.axis_index("z")

    def spread(x):
        return lax.all_to_all(x, plane, 0, 0, tiled=True)

    def shift(x, k):
        return lax.ppermute(x, "z", [(q, (q + k) % z_n) for q in range(z_n)])

    part = spread(pack(amplitudes, n, True)).reshape(shape)
    own = pack(amplitudes, n, False)
    tiles = [
        lax.dynamic_index_in_dim(part, lax.rem(z + k, z_n), 0, keepdims=False) for k in range(z_n)
    ]
    half = g_n // 2
    far = z_n // 2
    relay = shift(tiles[far][half:], far + 1)
    got = []
    for k in range(z_n):
        if k == 0:
            got.append([tiles[k]])
        elif k == far:
            got.append([shift(tiles[k][:half], k)])
        else:
            got.append([shift(tiles[k], k)])
    got[far].append(shift(relay, z_n - 1))
    base = add_term(exchange, amplitudes, fock_virt, over)
    base = add_term(base, amplitudes, over, fock_virt)
    own, _ = lax.optimization_barrier((own, tiles[0]))
    own = near(spread(own).reshape(shape))
    low, high = halo_columns(z, own, got)
    left = lax.ppermute(high, "z", [(k, k + 1) for k in range(z_n - 1)])
    right = lax.ppermute(low, "z", [(k + 1, k) for k in range(z_n - 1)])
    lists = partners.T
    weights = coupling.T
    middle, part = couple_inner(z, lists, weights, start_z[None], own, got, low, high)
    part = couple_edge(lists, weights, start_z[None], near(left), low, middle, high, near(right), part)
    coup = near(spread(part.reshape(n, rows, cols, width // n, width)))

    masks = jnp.repeat(domain.astype(jnp.float32), width // blocks, axis=1)
    mask_i = lax.dynamic_slice_in_dim(masks, start_i, rows, 0)
    mask_j = lax.dynamic_slice_in_dim(masks, start_j, cols, 0)
    occ = jnp.concatenate(
        [
            lax.dynamic_slice_in_dim(occ_energy, start_i, rows, 0),
            lax.dynamic_slice_in_dim(occ_energy, start_j, cols, 0),
        ]
    )
    return tuple(
        finish(occ, base, amplitudes, coup, mask_i, mask_j, over, transform, virt_energy)
    )


def solution(mesh):
    i_n, j_n = mesh.shape["occi"], mesh.shape["occj"]
    group = j_n // i_n
    z_n = j_n // group
    inner = Mesh(mesh.devices.reshape(i_n, z_n, group), ("a", "z", "g"))
    pairs = P("a", ("z", "g"), None, None)
    return jax.shard_map(
        per_device,
        mesh=inner,
        in_specs=(pairs, pairs, P(), P(), P(), P(), P(), P(), P(), P()),
        out_specs=(pairs, pairs),
        check_vma=False,
    )
```

```python
import functools

import jax
import jax.numpy as jnp
from jax import lax
from jax.experimental import pallas as pl
from jax.experimental.pallas import tpu as pltpu
from jax.sharding import Mesh
from jax.sharding import PartitionSpec as P

REACH = 2
VMEM = pl.BlockSpec(memory_space=pltpu.VMEM)
SMEM = pl.BlockSpec(memory_space=pltpu.SMEM)


def near(x):
    return pltpu.with_memory_space_constraint(x, pltpu.VMEM)


def pack_kernel(x_ref, o_ref, *, flip):
    n, _, _, sr, w = o_ref.shape
    for r in range(x_ref.shape[0]):
        for s in range(x_ref.shape[1]):
            block = x_ref[r, s]
            if flip:
                block = block.T
            o_ref[:, r, s] = block.reshape(n, sr, w)


def pack(x, n, flip):
    rows, cols, w, _ = x.shape
    sr = w // n
    step = 4
    return pl.pallas_call(
        functools.partial(pack_kernel, flip=flip),
        grid=(rows // step,),
        in_specs=[pl.BlockSpec((step, cols, w, w), lambda k: (k, 0, 0, 0))],
        out_specs=pl.BlockSpec((n, step, cols, sr, w), lambda k: (0, k, 0, 0, 0)),
        out_shape=jax.ShapeDtypeStruct((n, rows, cols, sr, w), jnp.bfloat16),
        name="pack_flip" if flip else "pack",
    )(x)


def _mirrored(got, split, k, j, i, g_n, s_n):
    at = sum(split[:k])
    parts = split[k]
    g = i // s_n
    return got[at + g * parts // g_n][g % (g_n // parts), j, i % s_n]


def _sym(own, mir):
    return (0.5 * (own.astype(jnp.float32) + mir.astype(jnp.float32))).astype(jnp.bfloat16)


def halo_kernel(z_ref, a_ref, *refs, split):
    got, (lo_ref, hi_ref) = refs[:-2], refs[-2:]
    t_n, g_n, r_n, s_n, _, _ = a_ref.shape
    j_n = g_n * s_n
    for k in range(t_n):
        t = lax.rem(z_ref[0] + (t_n - k), t_n)
        for o_ref, base in ((lo_ref, 0), (hi_ref, j_n - REACH)):
            for c in range(REACH):
                j = base + c
                for i in range(r_n):
                    mir = _mirrored(got, split, k, j, i, g_n, s_n)
                    o_ref[c, t * r_n + i] = _sym(a_ref[t, j // s_n, i, j % s_n], mir)


def _mix(weights_ref, at, x0, x1):
    total = weights_ref[0, at] * x0.astype(jnp.float32)
    return (total + weights_ref[1, at] * x1.astype(jnp.float32)).astype(jnp.bfloat16)


def inner_kernel(
    z_ref, lists_ref, weights_ref, start_ref, a_ref, lo_ref, hi_ref, *refs, split
):
    got, (mid_ref, o_ref, all_ref) = refs[:-3], refs[-3:]
    t_n, g_n, r_n, s_n, _, _ = a_ref.shape
    j_n = g_n * s_n
    start = start_ref[0]
    all_ref[0:REACH] = lo_ref[...]
    all_ref[j_n - REACH :] = hi_ref[...]
    for k in range(t_n):
        t = lax.rem(z_ref[0] + (t_n - k), t_n)
        for j in range(REACH, j_n - REACH):
            for i in range(r_n):
                mir = _mirrored(got, split, k, j, i, g_n, s_n)
                val = _sym(a_ref[t, j // s_n, i, j % s_n], mir)
                all_ref[j, t * r_n + i] = val
                mid_ref[j - REACH, t * r_n + i] = val

    def tile(t, carry):
        for j in range(j_n):
            gj = start + j
            for r in range(r_n):
                i = t * r_n + r
                out = _mix(weights_ref, i, all_ref[j, lists_ref[0, i]], all_ref[j, lists_ref[1, i]])
                if REACH <= j < j_n - REACH:
                    x0 = all_ref[lists_ref[0, gj] - start, i]
                    x1 = all_ref[lists_ref[1, gj] - start, i]
                    col = _mix(weights_ref, gj, x0, x1)
                    out = (out.astype(jnp.float32) + col.astype(jnp.float32)).astype(jnp.bfloat16)
                o_ref[t, j // s_n, r, j % s_n] = out
        return carry

    lax.fori_loop(0, t_n, tile, 0)


def edge_kernel(
    lists_ref, weights_ref, start_ref, left_ref, lo_ref, mid_ref, hi_ref, right_ref, x_ref, o_ref, ext_ref, sems
):
    t_n, _, r_n, s_n, _, _ = o_ref.shape
    k = pl.program_id(0)
    per = REACH // s_n
    start = start_ref[0]
    copies = []
    at = 0
    for ref, q0, n in (
        (left_ref, 0, REACH),
        (lo_ref, 0, REACH),
        (mid_ref, 0, REACH),
        (mid_ref, REACH, REACH),
        (hi_ref, 0, REACH),
        (right_ref, 0, REACH),
    ):
        src = ref.at[pl.ds(q0, n)]
        copies.append(pltpu.make_async_copy(src, ext_ref.at[pl.ds(at, n)], sems.at[len(copies)]))
        at += n

    @pl.when(k == 0)
    def _():
        for c in copies:
            c.start()
        for c in copies[:3]:
            c.wait()

    @pl.when(k == per)
    def _():
        for c in copies[3:]:
            c.wait()

    high = k >= per
    j0 = k * s_n
    gap = mid_ref.shape[0] - 2 * REACH
    gj0 = start + j0 + jnp.where(high, mid_ref.shape[0], 0)
    base = start - REACH + jnp.where(high, gap, 0)

    def tile(t, carry):
        for s in range(s_n):
            gj = gj0 + s
            for r in range(r_n):
                i = t * r_n + r
                col = _mix(
                    weights_ref,
                    gj,
                    ext_ref[lists_ref[0, gj] - base, i],
                    ext_ref[lists_ref[1, gj] - base, i],
                )
                row = x_ref[t, 0, r, s].astype(jnp.float32)
                o_ref[t, 0, r, s] = (row + col.astype(jnp.float32)).astype(jnp.bfloat16)
        return carry

    lax.fori_loop(0, t_n, tile, 0)


def halo_columns(z, own, got):
    t_n, _, r_n, _, sr, sl = own.shape
    split = [len(tile) for tile in got]
    flat = [part for tile in got for part in tile]
    return pl.pallas_call(
        functools.partial(halo_kernel, split=split),
        in_specs=[SMEM, VMEM] + [VMEM] * len(flat),
        out_specs=[VMEM] * 2,
        out_shape=[jax.ShapeDtypeStruct((REACH, t_n * r_n, sr, sl), jnp.bfloat16)] * 2,
        name="halo",
    )(z[None], own, *flat)


def couple_inner(z, lists, weights, start, own, got, low, high):
    t_n, g_n, r_n, s_n, sr, sl = own.shape
    j_n = g_n * s_n
    split = [len(tile) for tile in got]
    flat = [part for tile in got for part in tile]
    columns = lambda n: (n, t_n * r_n, sr, sl)
    return pl.pallas_call(
        functools.partial(inner_kernel, split=split),
        in_specs=[SMEM] * 4 + [VMEM] * (3 + len(flat)),
        out_specs=[VMEM] * 2,
        out_shape=[
            jax.ShapeDtypeStruct(columns(j_n - 2 * REACH), jnp.bfloat16),
            jax.ShapeDtypeStruct(own.shape, jnp.bfloat16),
        ],
        scratch_shapes=[pltpu.VMEM(columns(j_n), jnp.bfloat16)],
        name="inner",
    )(z[None], lists, weights, start, own, low, high, *flat)


def couple_edge(lists, weights, start, left, low, middle, high, right, part):
    t_n, g_n, r_n, s_n, sr, sl = part.shape
    per = REACH // s_n
    i_n = t_n * r_n
    hbm = pl.BlockSpec(memory_space=pl.ANY)
    block = pl.BlockSpec(
        (t_n, 1, r_n, s_n, sr, sl),
        lambda k: (0, k + jnp.where(k >= per, g_n - 2 * per, 0), 0, 0, 0, 0),
    )
    return pl.pallas_call(
        edge_kernel,
        grid=(2 * per,),
        in_specs=[SMEM, SMEM, SMEM, VMEM, hbm, hbm, hbm, VMEM, block],
        out_specs=block,
        out_shape=jax.ShapeDtypeStruct(part.shape, jnp.bfloat16),
        scratch_shapes=[
            pltpu.VMEM((6 * REACH, i_n, sr, sl), jnp.bfloat16),
            pltpu.SemaphoreType.DMA((6,)),
        ],
        input_output_aliases={8: 0},
        name="edge",
    )(lists, weights, start, left, low, middle, high, right, part)


def _dot(x, y):
    return jnp.dot(x, y, preferred_element_type=jnp.float32)


def pre_kernel(x_ref, amp_ref, left_ref, right_ref, o_ref):
    left = left_ref[...]
    right = right_ref[...]
    for s in range(amp_ref.shape[1]):
        term = _dot(_dot(left, amp_ref[0, s]).astype(jnp.bfloat16), right)
        o_ref[0, s] = x_ref[0, s].astype(jnp.float32) + term


def add_term(x, amp, left, right):
    rows, cols, w, _ = amp.shape
    big = pl.BlockSpec((1, cols, w, w), lambda k: (k, 0, 0, 0))
    mat = pl.BlockSpec((w, w), lambda k: (0, 0))
    return pl.pallas_call(
        pre_kernel,
        grid=(rows,),
        in_specs=[big, big, mat, mat],
        out_specs=big,
        out_shape=jax.ShapeDtypeStruct(amp.shape, jnp.float32),
        name="term",
    )(x, amp, left, right)


def post_kernel(
    occ_ref,
    base_ref,
    amp_ref,
    mask_i_ref,
    mask_j_ref,
    over_ref,
    trans_ref,
    tt_ref,
    energy_ref,
    coup_ref,
    res_ref,
    new_ref,
):
    k = pl.program_id(0)
    step, cols, w, _ = amp_ref.shape
    rows = pl.num_programs(0) * step
    over = over_ref[...]
    trans = trans_ref[...]
    tt = tt_ref[...]
    pairs = [(r, s) for r in range(step) for s in range(cols)]
    bf = lambda xs: [x.astype(jnp.bfloat16) for x in xs]

    def left(m, xs):
        return [_dot(m, x) for x in xs]

    def right(xs, m):
        return [_dot(x, m) for x in xs]

    marks = []
    b1 = []
    for r, s in pairs:
        mark = jnp.maximum(mask_i_ref[r], mask_j_ref[s])
        marks.append(mark)
        coup = coup_ref[:, k * step + r, s].reshape(w, w)
        b1.append(_dot((over.astype(jnp.float32) * mark).astype(jnp.bfloat16), coup) * mark)
    third = right(bf(b1), over)
    res = [(base_ref[r, s] - t) * m * m.T for m, t, (r, s) in zip(marks, third, pairs)]
    for x, (r, s) in zip(res, pairs):
        res_ref[r, s] = x
    q = right(bf(left(tt, bf(res))), trans)
    energy = energy_ref[...].T + energy_ref[...]
    z = [
        x / (energy - (occ_ref[k * step + r] + occ_ref[rows + s])) for x, (r, s) in zip(q, pairs)
    ]
    u = right(bf(left(trans, bf(z))), tt)
    for x, (r, s) in zip(u, pairs):
        new_ref[r, s] = (amp_ref[r, s].astype(jnp.float32) - x).astype(jnp.bfloat16)


def finish(occ, base, amp, coup, mask_i, mask_j, over, trans, energy):
    rows, cols, w, _ = amp.shape
    step = 4
    big = pl.BlockSpec((step, cols, w, w), lambda k, *_: (k, 0, 0, 0))
    mat = pl.BlockSpec((w, w), lambda k, *_: (0, 0))
    return pl.pallas_call(
        post_kernel,
        grid_spec=pltpu.PrefetchScalarGridSpec(
            num_scalar_prefetch=1,
            grid=(rows // step,),
            in_specs=[
                big,
                big,
                pl.BlockSpec((step, 1, w), lambda k, *_: (k, 0, 0)),
                pl.BlockSpec((cols, 1, w), lambda k, *_: (0, 0, 0)),
                mat,
                mat,
                mat,
                pl.BlockSpec((1, w), lambda k, *_: (0, 0)),
                VMEM,
            ],
            out_specs=[big, big],
        ),
        out_shape=[
            jax.ShapeDtypeStruct(amp.shape, jnp.float32),
            jax.ShapeDtypeStruct(amp.shape, jnp.bfloat16),
        ],
        name="finish",
    )(
        occ,
        base,
        amp,
        mask_i[:, None, :],
        mask_j[:, None, :],
        over,
        trans,
        trans.T,
        energy[None, :],
        coup,
    )


def per_device(
    amplitudes,
    exchange,
    fock_virt,
    intersection,
    transform,
    virt_energy,
    occ_energy,
    partners,
    coupling,
    domain,
):
    rows, cols, width, _ = amplitudes.shape
    blocks = domain.shape[1]
    a_n = lax.axis_size("a")
    z_n = lax.axis_size("z")
    g_n = lax.axis_size("g")
    start_i = lax.axis_index("a") * rows
    start_z = lax.axis_index("z") * (g_n * cols)
    start_j = start_z + lax.axis_index("g") * cols
    plane = ("a", "g")
    n = a_n * g_n

    over = (jnp.eye(width, dtype=jnp.float32) + intersection.astype(jnp.float32)).astype(
        jnp.bfloat16
    )
    shape = (a_n, g_n, rows, cols, width // n, width)
    z = lax.axis_index("z")

    def spread(x):
        return lax.all_to_all(x, plane, 0, 0, tiled=True)

    def shift(x, k):
        return lax.ppermute(x, "z", [(q, (q + k) % z_n) for q in range(z_n)])

    part = spread(pack(amplitudes, n, True)).reshape(shape)
    own = pack(amplitudes, n, False)
    tiles = [
        lax.dynamic_index_in_dim(part, lax.rem(z + k, z_n), 0, keepdims=False) for k in range(z_n)
    ]
    half = g_n // 2
    far = z_n // 2
    relay = shift(tiles[far][half:], far + 1)
    got = []
    for k in range(z_n):
        if k == 0:
            got.append([tiles[k]])
        elif k == far:
            got.append([shift(tiles[k][:half], k)])
        else:
            got.append([shift(tiles[k], k)])
    got[far].append(shift(relay, z_n - 1))
    base = add_term(exchange, amplitudes, fock_virt, over)
    base = add_term(base, amplitudes, over, fock_virt)
    own, _ = lax.optimization_barrier((own, tiles[0]))
    own = near(spread(own).reshape(shape))
    low, high = halo_columns(z, own, got)
    left = lax.ppermute(high, "z", [(k, k + 1) for k in range(z_n - 1)])
    right = lax.ppermute(low, "z", [(k + 1, k) for k in range(z_n - 1)])
    lists = partners.T
    weights = coupling.T
    middle, part = couple_inner(z, lists, weights, start_z[None], own, got, low, high)
    part = couple_edge(lists, weights, start_z[None], near(left), low, middle, high, near(right), part)
    coup = near(spread(part.reshape(n, rows, cols, width // n, width)))

    masks = jnp.repeat(domain.astype(jnp.float32), width // blocks, axis=1)
    mask_i = lax.dynamic_slice_in_dim(masks, start_i, rows, 0)
    mask_j = lax.dynamic_slice_in_dim(masks, start_j, cols, 0)
    occ = jnp.concatenate(
        [
            lax.dynamic_slice_in_dim(occ_energy, start_i, rows, 0),
            lax.dynamic_slice_in_dim(occ_energy, start_j, cols, 0),
        ]
    )
    return tuple(
        finish(occ, base, amplitudes, coup, mask_i, mask_j, over, transform, virt_energy)
    )


def solution(mesh):
    i_n, j_n = mesh.shape["occi"], mesh.shape["occj"]
    group = j_n // i_n
    z_n = j_n // group
    inner = Mesh(mesh.devices.reshape(i_n, z_n, group), ("a", "z", "g"))
    pairs = P("a", ("z", "g"), None, None)
    return jax.shard_map(
        per_device,
        mesh=inner,
        in_specs=(pairs, pairs, P(), P(), P(), P(), P(), P(), P(), P()),
        out_specs=(pairs, pairs),
        check_vma=False,
    )
```

```python
import functools

import jax
import jax.numpy as jnp
from jax import lax
from jax.experimental import pallas as pl
from jax.experimental.pallas import tpu as pltpu
from jax.sharding import Mesh
from jax.sharding import PartitionSpec as P

REACH = 2
VMEM = pl.BlockSpec(memory_space=pltpu.VMEM)
SMEM = pl.BlockSpec(memory_space=pltpu.SMEM)
GRANT = pltpu.CompilerParams(vmem_limit_bytes=52 * 1024 * 1024)


def near(x):
    return pltpu.with_memory_space_constraint(x, pltpu.VMEM)


def pack_kernel(x_ref, o_ref, *, flip):
    n, _, _, sr, w = o_ref.shape
    for r in range(x_ref.shape[0]):
        for s in range(x_ref.shape[1]):
            block = x_ref[r, s]
            if flip:
                block = block.T
            o_ref[:, r, s] = block.reshape(n, sr, w)


def pack(x, n, flip):
    rows, cols, w, _ = x.shape
    sr = w // n
    step = 4
    return pl.pallas_call(
        functools.partial(pack_kernel, flip=flip),
        grid=(rows // step,),
        in_specs=[pl.BlockSpec((step, cols, w, w), lambda k: (k, 0, 0, 0))],
        out_specs=pl.BlockSpec((n, step, cols, sr, w), lambda k: (0, k, 0, 0, 0)),
        out_shape=jax.ShapeDtypeStruct((n, rows, cols, sr, w), jnp.bfloat16),
        name="pack_flip" if flip else "pack",
    )(x)


def _mirrored(got, split, k, j, i, g_n, s_n):
    at = sum(split[:k])
    parts = split[k]
    g = i // s_n
    return got[at + g * parts // g_n][g % (g_n // parts), j, i % s_n]


def _sym(own, mir):
    return (0.5 * (own.astype(jnp.float32) + mir.astype(jnp.float32))).astype(jnp.bfloat16)


def halo_kernel(z_ref, a_ref, *refs, split):
    got, (lo_ref, hi_ref) = refs[:-2], refs[-2:]
    t_n, g_n, r_n, s_n, _, _ = a_ref.shape
    j_n = g_n * s_n
    for k in range(t_n):
        t = lax.rem(z_ref[0] + (t_n - k), t_n)
        for o_ref, base in ((lo_ref, 0), (hi_ref, j_n - REACH)):
            for c in range(REACH):
                j = base + c
                for i in range(r_n):
                    mir = _mirrored(got, split, k, j, i, g_n, s_n)
                    o_ref[c, t * r_n + i] = _sym(a_ref[t, j // s_n, i, j % s_n], mir)


def _mix(weights_ref, at, x0, x1):
    total = weights_ref[0, at] * x0.astype(jnp.float32)
    return (total + weights_ref[1, at] * x1.astype(jnp.float32)).astype(jnp.bfloat16)


def inner_kernel(
    z_ref, lists_ref, weights_ref, start_ref, a_ref, lo_ref, hi_ref, *refs, split
):
    got, (ext_ref, row_ref, o_ref) = refs[:-3], refs[-3:]
    t_n, g_n, r_n, s_n, _, _ = a_ref.shape
    j_n = g_n * s_n
    per = REACH // s_n
    base = start_ref[0] - REACH
    ext_ref[REACH : 2 * REACH] = lo_ref[...]
    ext_ref[j_n : j_n + REACH] = hi_ref[...]
    for k in range(t_n):
        t = lax.rem(z_ref[0] + (t_n - k), t_n)
        for j in range(REACH, j_n - REACH):
            for i in range(r_n):
                mir = _mirrored(got, split, k, j, i, g_n, s_n)
                ext_ref[j + REACH, t * r_n + i] = _sym(a_ref[t, j // s_n, i, j % s_n], mir)

    def tile(t, carry):
        for j in range(j_n):
            gj = start_ref[0] + j
            g, s = j // s_n, j % s_n
            for r in range(r_n):
                i = t * r_n + r
                x0 = ext_ref[j + REACH, lists_ref[0, i]]
                x1 = ext_ref[j + REACH, lists_ref[1, i]]
                out = _mix(weights_ref, i, x0, x1)
                if REACH <= j < j_n - REACH:
                    x0 = ext_ref[lists_ref[0, gj] - base, i]
                    x1 = ext_ref[lists_ref[1, gj] - base, i]
                    col = _mix(weights_ref, gj, x0, x1)
                    out = (out.astype(jnp.float32) + col.astype(jnp.float32)).astype(jnp.bfloat16)
                    o_ref[t, g, r, s] = out
                else:
                    row_ref[t, g if g < per else g - (g_n - 2 * per), r, s] = out
        return carry

    lax.fori_loop(0, t_n, tile, 0)


def edge_kernel(
    lists_ref, weights_ref, start_ref, left_ref, right_ref, row_ref, _, __, ext_ref, o_ref
):
    t_n, _, r_n, s_n, _, _ = o_ref.shape
    j_n = ext_ref.shape[0] - 2 * REACH
    per = REACH // s_n
    k = pl.program_id(0)
    base = start_ref[0] - REACH
    gj0 = start_ref[0] + k * s_n + jnp.where(k >= per, j_n - 2 * REACH, 0)

    @pl.when(k == 0)
    def _():
        ext_ref[0:REACH] = left_ref[...]
        ext_ref[j_n + REACH :] = right_ref[...]

    def tile(t, carry):
        for s in range(s_n):
            gj = gj0 + s
            for r in range(r_n):
                i = t * r_n + r
                x0 = ext_ref[lists_ref[0, gj] - base, i]
                x1 = ext_ref[lists_ref[1, gj] - base, i]
                col = _mix(weights_ref, gj, x0, x1).astype(jnp.float32)
                row = row_ref[t, k, r, s].astype(jnp.float32)
                o_ref[t, 0, r, s] = (row + col).astype(jnp.bfloat16)
        return carry

    lax.fori_loop(0, t_n, tile, 0)


def halo_columns(z, own, got):
    t_n, _, r_n, _, sr, sl = own.shape
    split = [len(tile) for tile in got]
    flat = [part for tile in got for part in tile]
    return pl.pallas_call(
        functools.partial(halo_kernel, split=split),
        in_specs=[SMEM, VMEM] + [VMEM] * len(flat),
        out_specs=[VMEM] * 2,
        out_shape=[jax.ShapeDtypeStruct((REACH, t_n * r_n, sr, sl), jnp.bfloat16)] * 2,
        name="halo",
    )(z[None], own, *flat)


def couple_inner(z, lists, weights, start, own, got, low, high):
    t_n, g_n, r_n, s_n, sr, sl = own.shape
    split = [len(tile) for tile in got]
    flat = [part for tile in got for part in tile]
    return pl.pallas_call(
        functools.partial(inner_kernel, split=split),
        in_specs=[SMEM] * 4 + [VMEM] * (3 + len(flat)),
        out_specs=[VMEM] * 3,
        out_shape=[
            pltpu.VMEM((g_n * s_n + 2 * REACH, t_n * r_n, sr, sl), jnp.bfloat16),
            pltpu.VMEM((t_n, 2 * REACH // s_n, r_n, s_n, sr, sl), jnp.bfloat16),
            jax.ShapeDtypeStruct(own.shape, jnp.bfloat16),
        ],
        compiler_params=GRANT,
        name="inner",
    )(z[None], lists, weights, start, own, low, high, *flat)


def couple_edge(lists, weights, start, left, right, ext, row, part):
    t_n, g_n, r_n, s_n, sr, sl = part.shape
    per = REACH // s_n
    block = pl.BlockSpec(
        (t_n, 1, r_n, s_n, sr, sl),
        lambda k: (0, k + jnp.where(k >= per, g_n - 2 * per, 0), 0, 0, 0, 0),
    )
    return pl.pallas_call(
        edge_kernel,
        grid=(2 * per,),
        in_specs=[SMEM] * 3 + [VMEM] * 4 + [pl.BlockSpec(memory_space=pl.ANY)],
        out_specs=[VMEM, block],
        out_shape=[
            pltpu.VMEM(ext.shape, ext.dtype),
            jax.ShapeDtypeStruct(part.shape, part.dtype),
        ],
        input_output_aliases={6: 0, 7: 1},
        compiler_params=GRANT,
        name="edge",
    )(lists, weights, start, left, right, row, ext, part)[1]


def _dot(x, y):
    return jnp.dot(x, y, preferred_element_type=jnp.float32)


def pre_kernel(x_ref, amp_ref, left_ref, right_ref, o_ref):
    left = left_ref[...]
    right = right_ref[...]
    for s in range(amp_ref.shape[1]):
        term = _dot(_dot(left, amp_ref[0, s]).astype(jnp.bfloat16), right)
        o_ref[0, s] = x_ref[0, s].astype(jnp.float32) + term


def add_term(x, amp, left, right):
    rows, cols, w, _ = amp.shape
    big = pl.BlockSpec((1, cols, w, w), lambda k: (k, 0, 0, 0))
    mat = pl.BlockSpec((w, w), lambda k: (0, 0))
    return pl.pallas_call(
        pre_kernel,
        grid=(rows,),
        in_specs=[big, big, mat, mat],
        out_specs=big,
        out_shape=jax.ShapeDtypeStruct(amp.shape, jnp.float32),
        name="term",
    )(x, amp, left, right)


def post_kernel(
    occ_ref,
    base_ref,
    amp_ref,
    mask_i_ref,
    mask_j_ref,
    over_ref,
    trans_ref,
    tt_ref,
    energy_ref,
    coup_ref,
    res_ref,
    new_ref,
):
    k = pl.program_id(0)
    step, cols, w, _ = amp_ref.shape
    rows = pl.num_programs(0) * step
    over = over_ref[...]
    trans = trans_ref[...]
    tt = tt_ref[...]
    pairs = [(r, s) for r in range(step) for s in range(cols)]
    bf = lambda xs: [x.astype(jnp.bfloat16) for x in xs]

    def left(m, xs):
        return [_dot(m, x) for x in xs]

    def right(xs, m):
        return [_dot(x, m) for x in xs]

    marks = []
    b1 = []
    for r, s in pairs:
        mark = jnp.maximum(mask_i_ref[r], mask_j_ref[s])
        marks.append(mark)
        coup = coup_ref[:, k * step + r, s].reshape(w, w)
        b1.append(_dot((over.astype(jnp.float32) * mark).astype(jnp.bfloat16), coup) * mark)
    third = right(bf(b1), over)
    res = [(base_ref[r, s] - t) * m * m.T for m, t, (r, s) in zip(marks, third, pairs)]
    for x, (r, s) in zip(res, pairs):
        res_ref[r, s] = x
    q = right(bf(left(tt, bf(res))), trans)
    energy = energy_ref[...].T + energy_ref[...]
    z = [
        x / (energy - (occ_ref[k * step + r] + occ_ref[rows + s])) for x, (r, s) in zip(q, pairs)
    ]
    u = right(bf(left(trans, bf(z))), tt)
    for x, (r, s) in zip(u, pairs):
        new_ref[r, s] = (amp_ref[r, s].astype(jnp.float32) - x).astype(jnp.bfloat16)


def finish(occ, base, amp, coup, mask_i, mask_j, over, trans, energy):
    rows, cols, w, _ = amp.shape
    step = 4
    big = pl.BlockSpec((step, cols, w, w), lambda k, *_: (k, 0, 0, 0))
    mat = pl.BlockSpec((w, w), lambda k, *_: (0, 0))
    return pl.pallas_call(
        post_kernel,
        grid_spec=pltpu.PrefetchScalarGridSpec(
            num_scalar_prefetch=1,
            grid=(rows // step,),
            in_specs=[
                big,
                big,
                pl.BlockSpec((step, 1, w), lambda k, *_: (k, 0, 0)),
                pl.BlockSpec((cols, 1, w), lambda k, *_: (0, 0, 0)),
                mat,
                mat,
                mat,
                pl.BlockSpec((1, w), lambda k, *_: (0, 0)),
                VMEM,
            ],
            out_specs=[big, big],
        ),
        out_shape=[
            jax.ShapeDtypeStruct(amp.shape, jnp.float32),
            jax.ShapeDtypeStruct(amp.shape, jnp.bfloat16),
        ],
        name="finish",
    )(
        occ,
        base,
        amp,
        mask_i[:, None, :],
        mask_j[:, None, :],
        over,
        trans,
        trans.T,
        energy[None, :],
        coup,
    )


def per_device(
    amplitudes,
    exchange,
    fock_virt,
    intersection,
    transform,
    virt_energy,
    occ_energy,
    partners,
    coupling,
    domain,
):
    rows, cols, width, _ = amplitudes.shape
    blocks = domain.shape[1]
    a_n = lax.axis_size("a")
    z_n = lax.axis_size("z")
    g_n = lax.axis_size("g")
    start_i = lax.axis_index("a") * rows
    start_z = lax.axis_index("z") * (g_n * cols)
    start_j = start_z + lax.axis_index("g") * cols
    plane = ("a", "g")
    n = a_n * g_n

    over = (jnp.eye(width, dtype=jnp.float32) + intersection.astype(jnp.float32)).astype(
        jnp.bfloat16
    )
    shape = (a_n, g_n, rows, cols, width // n, width)
    z = lax.axis_index("z")

    def spread(x):
        return lax.all_to_all(x, plane, 0, 0, tiled=True)

    def shift(x, k):
        return lax.ppermute(x, "z", [(q, (q + k) % z_n) for q in range(z_n)])

    part = spread(pack(amplitudes, n, True)).reshape(shape)
    own = pack(amplitudes, n, False)
    tiles = [
        lax.dynamic_index_in_dim(part, lax.rem(z + k, z_n), 0, keepdims=False) for k in range(z_n)
    ]
    half = g_n // 2
    far = z_n // 2
    relay = shift(tiles[far][half:], far + 1)
    got = []
    for k in range(z_n):
        if k == 0:
            got.append([tiles[k]])
        elif k == far:
            got.append([shift(tiles[k][:half], k)])
        else:
            got.append([shift(tiles[k], k)])
    got[far].append(shift(relay, z_n - 1))
    base = add_term(exchange, amplitudes, fock_virt, over)
    base = add_term(base, amplitudes, over, fock_virt)
    own, _ = lax.optimization_barrier((own, tiles[0]))
    own = near(spread(own).reshape(shape))
    low, high = halo_columns(z, own, got)
    left = lax.ppermute(high, "z", [(k, k + 1) for k in range(z_n - 1)])
    right = lax.ppermute(low, "z", [(k + 1, k) for k in range(z_n - 1)])
    lists = partners.T
    weights = coupling.T
    ext, row, part = couple_inner(z, lists, weights, start_z[None], own, got, low, high)
    part = couple_edge(lists, weights, start_z[None], near(left), near(right), ext, near(row), part)
    coup = near(spread(part.reshape(n, rows, cols, width // n, width)))

    masks = jnp.repeat(domain.astype(jnp.float32), width // blocks, axis=1)
    mask_i = lax.dynamic_slice_in_dim(masks, start_i, rows, 0)
    mask_j = lax.dynamic_slice_in_dim(masks, start_j, cols, 0)
    occ = jnp.concatenate(
        [
            lax.dynamic_slice_in_dim(occ_energy, start_i, rows, 0),
            lax.dynamic_slice_in_dim(occ_energy, start_j, cols, 0),
        ]
    )
    return tuple(
        finish(occ, base, amplitudes, coup, mask_i, mask_j, over, transform, virt_energy)
    )


def solution(mesh):
    i_n, j_n = mesh.shape["occi"], mesh.shape["occj"]
    group = j_n // i_n
    z_n = j_n // group
    inner = Mesh(mesh.devices.reshape(i_n, z_n, group), ("a", "z", "g"))
    pairs = P("a", ("z", "g"), None, None)
    return jax.shard_map(
        per_device,
        mesh=inner,
        in_specs=(pairs, pairs, P(), P(), P(), P(), P(), P(), P(), P()),
        out_specs=(pairs, pairs),
        check_vma=False,
    )
```
